128 devices in a mesh: gx: 8 (over x, core), gy: 16 (over y, z).
Axes of the slice: x: 4, y: 4, z: 4, core: 2. Of those that a mesh axis runs over, the one named last changes fastest.
Arguments:
- flux: float32 [8, 512, 4096], P(None, 'gx', 'gy'), may hold values from -6 to 6
- diffusivity: float32 [256, 2048], P('gx', 'gy'), may hold values from 0.08 to 0.24
- remap_bank: bfloat16 [16, 3, 256, 128], replicated, may hold values from -0.21875 to 0.21875
- rec_owner: int32 [16384], P(('gx', 'gy')), may hold values from 0 to 127, as said below
- rec_source: int32 [16384], P(('gx', 'gy')), may hold values from 0 to 63
- rec_target: int32 [16384], P(('gx', 'gy')), may hold values from 0 to 31
- rec_weight: int32 [16384], P(('gx', 'gy')), may hold values from 0 to 15
Outputs:
- ocean_state: float32 [8, 256, 2048], P(None, 'gx', 'gy')
The draws below stay inside these ranges and needn't reach their ends.
Inputs may be any that keep to these rules, and one draw needn't show every extreme that they name: `rec_owner`: among the records of one atmosphere block each owner appears at most 2 times; in every draw some owner appears exactly 2 times in every block's records.
All inputs are finite; a program needn't handle non-finite values.
Results may differ from the reference program's by a relative error of at most 0.0029.
Values may be sent and summed in bfloat16 or wider, within the bound.
No kernel may reach another device: no remote copies, remote signals or barrier semaphores. Data moves between devices by JAX's collectives and lax.ppermute only.
A program may use at most 64 MiB of HBM per device.

```python
import math
import jax
import jax.numpy as jnp
from jax import lax

F = 8
TILE_X = 16
TILE_Y = 16
OTILE_X = 8
OTILE_Y = 16
NWB = 16
SWEEPS = 4
AXD = 64
AYD = 256
TC = 256
OC = 128
OXD = 32
OYD = 128
AX = 512
AY = 4096
OX = 256
OY = 2048
ST = 64
OT = 32
RECS = 128
OWNERS = 128
CAP = 2
RECORDS = 16384
N_GY = 16


def draw_rec_owner(key, part):
    slot_count = OWNERS * CAP
    bias_key, hot_key, source_key = jax.random.split(jax.random.fold_in(key, 11), 3)
    bias = jax.random.randint(bias_key, (OWNERS,), 0, 4)
    hot_owner = jax.random.randint(hot_key, (), 0, OWNERS)
    owner_of = jnp.arange(slot_count, dtype=jnp.int32) // CAP

    def one_source(index):
        noise_key, order_key = jax.random.split(jax.random.fold_in(source_key, index))
        noise = jax.random.randint(noise_key, (slot_count,), 0, 4096)
        lifted = jnp.where(owner_of == hot_owner, 65536, 0)
        score = (bias[owner_of] * 1024 + noise + lifted) * slot_count + jnp.arange(slot_count, dtype=jnp.int32)
        chosen = jnp.argsort(-score)[:RECS]
        picked = owner_of[chosen]
        return picked[jax.random.permutation(order_key, RECS)]
    return jax.vmap(one_source)(jnp.arange(OWNERS)).reshape(-1).astype(jnp.int32)


def plant(result, key, least, largest):
    longest = result.shape.index(max(result.shape))
    spots = []
    for shift in (0, 1):
        where = [jax.random.randint(jax.random.fold_in(key, axis), (), 0, length) for axis, length in enumerate(result.shape)]
        where[longest] = (where[longest] + shift) % result.shape[longest]
        spots.append(tuple(where))
    return result.at[spots[0]].set(least).at[spots[1]].set(largest)


def levels(own_key, extent, cuts, low, largest):
    loudness = 1.0
    for axis_at, blocks in cuts:
        draws = jax.random.uniform(jax.random.fold_in(jax.random.fold_in(own_key, 6), axis_at), (blocks,), jnp.float32, low / len(cuts), largest / len(cuts))
        loudness = loudness * jnp.repeat(jnp.exp(draws), extent[axis_at] // blocks).reshape((-1,) + (1,) * (len(extent) - 1 - axis_at))
    return loudness


def normal_values(key, shape, spread, limit, cuts=(), kind=jnp.bfloat16):
    array = jax.random.normal(key, shape, jnp.float32) * spread
    if len(cuts) > 0:
        array = levels(key, shape, cuts, -0.22, 0.18) * array
    return jnp.clip(array, min=-limit, max=limit).astype(kind)


def setup_inputs(seed: int = 0) -> dict:
    splits = jax.random.split(jax.random.key(seed), 8)
    return {
        "flux": normal_values(splits[0], (F, AX, AY), 1.0, 6.0, ((1, 8), (2, 16)), jnp.float32),
        "diffusivity": jnp.clip(jnp.exp(math.log(0.24) - 1.0986123 * jax.random.uniform(splits[1], (OX, OY), jnp.float32) ** levels(splits[1], (OX, OY), ((0, 8), (1, 16)), -0.2, 0.2)), 0.08, 0.24),
        "remap_bank": normal_values(splits[2], (NWB, 3, TC, OC), (3 * TC) ** -0.5, 0.21875),
        "rec_owner": draw_rec_owner(jax.random.fold_in(splits[7], 71), 0),
        "rec_source": plant(jax.random.randint(splits[4], (RECORDS,), 0, ST), jax.random.fold_in(splits[4], 1), 0, ST - 1).astype(jnp.int32),
        "rec_target": plant(jax.random.randint(splits[5], (RECORDS,), 0, OT), jax.random.fold_in(splits[5], 1), 0, OT - 1).astype(jnp.int32),
        "rec_weight": plant(jax.random.randint(splits[6], (RECORDS,), 0, NWB), jax.random.fold_in(splits[6], 1), 0, NWB - 1).astype(jnp.int32),
    }


def reference(flux, diffusivity, remap_bank, rec_owner, rec_source, rec_target, rec_weight):
    slope_x = (jnp.roll(flux, -1, 1) - jnp.roll(flux, 1, 1)) * 0.5
    slope_y = (jnp.roll(flux, -1, 2) - jnp.roll(flux, 1, 2)) * 0.5
    coeffs = jnp.stack([flux, slope_x, slope_y]).astype(jnp.bfloat16)
    grid_tx = AX // TILE_X
    grid_ty = AY // TILE_Y
    all_tiles = coeffs.reshape(3, F, grid_tx, TILE_X, grid_ty, TILE_Y)
    all_tiles = all_tiles.transpose(2, 4, 0, 1, 3, 5).reshape(grid_tx * grid_ty, 3, F, TC)
    source_block = jnp.arange(RECORDS, dtype=jnp.int32) // RECS
    per_row = AYD // TILE_Y
    tile_i = (source_block // N_GY) * (AXD // TILE_X) + rec_source // per_row
    tile_j = (source_block % N_GY) * per_row + rec_source % per_row
    source_id = (tile_i * grid_ty + tile_j).astype(jnp.int32)
    ocean_tx = OX // OTILE_X
    ocean_ty = OY // OTILE_Y
    ocean_row = OYD // OTILE_Y
    target_i = (rec_owner // N_GY) * (OXD // OTILE_X) + rec_target // ocean_row
    target_j = (rec_owner % N_GY) * ocean_row + rec_target % ocean_row
    target_id = (target_i * ocean_ty + target_j).astype(jnp.int32)
    group_size = math.gcd(RECORDS, 64)
    block_count = RECORDS // group_size

    def accumulate(total, pieces):
        src_ids, weight_ids, dest_ids = pieces
        source_part = all_tiles[src_ids].astype(jnp.float32)
        bank_part = remap_bank[weight_ids].astype(jnp.float32)
        contribution = jnp.einsum("gkfc,gkco->gfo", source_part, bank_part, precision=lax.Precision.HIGHEST)
        return total.at[dest_ids].add(contribution), None

    start_total = jnp.zeros((ocean_tx * ocean_ty, F, OC), jnp.float32)
    forcing_tiles, unused = lax.scan(accumulate, start_total, (source_id.reshape(block_count, group_size), rec_weight.reshape(block_count, group_size), target_id.reshape(block_count, group_size)))
    forcing = forcing_tiles.reshape(ocean_tx, ocean_ty, F, OTILE_X, OTILE_Y)
    ocean = forcing.transpose(2, 0, 3, 1, 4).reshape(F, OX, OY)
    for sweep in range(SWEEPS):
        padded = jnp.pad(ocean, ((0, 0), (1, 1), (1, 1)))
        beside_all = padded[:, 2:, 1:-1] + padded[:, :-2, 1:-1] + padded[:, 1:-1, 2:] + padded[:, 1:-1, :-2]
        ocean = ocean + diffusivity * (beside_all - 4.0 * ocean)
    return ocean
```

```python
import jax
import jax.numpy as jnp
from jax import lax
from jax.experimental import pallas as pl
from jax.experimental.pallas import tpu as pltpu
from jax.sharding import PartitionSpec as P

F = 8
AXD, AYD = 64, 256
OXD, OYD = 32, 128
NWB = 16
RECS = 128
SWEEPS = 4
OWNERS = 128
NGX, NGY = 8, 16
(W, T8, OWN, SLOT, DX, DY, DC, MX, MY, MC, SHIFT, PO, PX, PY, VO, VX, VY, POS) = range(18)
ABSENT = 256.0


def lanes(shape):
    return lax.broadcasted_iota(jnp.int32, shape, 1)


def swap_blocks(v):
    block = lanes((8, 128)) // 16
    for s in range(3):
        d = 1 << s
        high = (block & d) != 0
        n = list(v)
        for p in range(8):
            if not p & d:
                a, b = v[p], v[p | d]
                n[p] = jnp.where(high, pltpu.roll(b, 16 * d, 1), a)
                n[p | d] = jnp.where(high, b, pltpu.roll(a, 128 - 16 * d, 1))
        v = n
    return v


def send_kernel(tab, flux_in, above, below, before, after, diff, bank, out, lhs, prod, stage, mask, flux, sems):
    copies = [pltpu.make_async_copy(flux_in.at[:, pl.ds(g * 128, 128)], flux.at[g], sems.at[g]) for g in range(2)]
    for copy in copies:
        copy.start()
    lane = lanes((8, 128))
    sub = lax.broadcasted_iota(jnp.int32, (8, 128), 0)
    a_of, b_of = lane // 16, lane % 16

    is_label = (a_of == 2) & (b_of >= 4) & (b_of < 12) | (a_of == 3) & (b_of >= 4) & (b_of < 6)
    empty = jnp.where(is_label, ABSENT, 0.0).astype(jnp.float32)
    zero = jnp.zeros((8, 128), jnp.float32)

    def clear(o, carry):
        for j in range(3):
            stage[o, j, 0:8, :] = zero
            stage[o, j, 8:16, :] = empty if j == 2 else zero
        return carry

    lax.fori_loop(0, OWNERS + 1, clear, 0, unroll=3)

    def put_mask(at, cond):
        mask[at] = cond.astype(jnp.float32)

    put_mask(0, lane < 64)
    put_mask(1, lane >= 64)
    put_mask(2, b_of < 4)
    put_mask(3, (b_of >= 4) & (b_of < 8))
    put_mask(4, b_of >= 12)
    put_mask(5, (b_of >= 8) & (b_of < 12))
    put_mask(6, (lane < 64) & (b_of < 4))
    put_mask(7, (lane < 64) & (b_of >= 12))
    put_mask(8, (lane >= 64) & (b_of < 4))
    put_mask(9, (lane >= 64) & (b_of >= 12))

    wide = lanes((8, 256))
    left, right = before[0:8, :], after[0:8, :]

    def row(i):
        if i < 0:
            return jnp.concatenate([above[0:8, :], above[8:16, :]], axis=1)
        if i >= AXD:
            return jnp.concatenate([below[0:8, :], below[8:16, :]], axis=1)
        return jnp.concatenate([flux[g, pl.ds(i, 8, stride=AXD), :] for g in range(2)], axis=1)

    for copy in copies:
        copy.wait()
    for ti in range(4):
        x = [row(i) for i in range(ti * 16 - 1, ti * 16 + 17)]
        for k in range(3):
            vals = []
            for a in range(16):
                i = ti * 16 + a
                if k == 0:
                    vals.append(x[a + 1])
                elif k == 1:
                    vals.append((x[a + 2] - x[a]) * 0.5)
                else:
                    nxt = jnp.where(wide == 255, right[:, i : i + 1], pltpu.roll(x[a + 1], 255, 1))
                    prv = jnp.where(wide == 0, left[:, i : i + 1], pltpu.roll(x[a + 1], 1, 1))
                    vals.append((nxt - prv) * 0.5)
            for h in range(2):
                y = [swap_blocks([vals[h * 8 + q][:, g * 128 : (g + 1) * 128] for q in range(8)]) for g in range(2)]
                for q in range(8):
                    lhs[pl.ds((ti * 8 + q) * 16, 16), pl.ds(k * 256 + h * 128, 128)] = jnp.concatenate(
                        [y[0][q], y[1][q]], axis=0
                    ).astype(jnp.bfloat16)

    def product(n, carry):
        rhs = jnp.concatenate([bank[2 * n], bank[2 * n + 1]], axis=1)
        res = jnp.dot(lhs[...], rhs, preferred_element_type=jnp.float32)
        prod[2 * n] = res[:, :128]
        prod[2 * n + 1] = res[:, 128:]
        return carry

    lax.fori_loop(0, NWB // 2, product, 0)

    def record(r, carry):
        c8 = pl.multiple_of(tab[SLOT, r] * 8, 8)
        own, dx, dy, dc = tab[OWN, r], tab[DX, r], tab[DY, r], tab[DC, r]
        value = prod[tab[W, r], pl.ds(pl.multiple_of(tab[T8, r], 8), 8), :]
        stage[own, 0, pl.ds(c8, 8), :] = value
        stage[dx, 1, pl.ds(c8, 8), :] = jnp.where(mask[tab[MX, r]] > 0, value, stage[dx, 1, pl.ds(c8, 8), :])
        turned = pltpu.roll(value, tab[SHIFT, r], 1)
        stage[dy, 2, 0:8, :] = jnp.where(mask[tab[MY, r]] > 0, turned, stage[dy, 2, 0:8, :])
        stage[own, 2, 8:16, :] = jnp.where(lane == tab[PO, r], (sub + tab[VO, r]).astype(jnp.float32), stage[own, 2, 8:16, :])
        stage[dx, 2, 8:16, :] = jnp.where(lane == tab[PX, r], (sub + tab[VX, r]).astype(jnp.float32), stage[dx, 2, 8:16, :])
        stage[dy, 2, 8:16, :] = jnp.where(lane == tab[PY, r], (sub + tab[VY, r]).astype(jnp.float32), stage[dy, 2, 8:16, :])
        stage[dc, 2, 8:16, :] = stage[dc, 2, 8:16, :] + jnp.where(mask[tab[MC, r]] > 0, value, 0.0)
        return carry

    lax.fori_loop(0, RECS, record, 0, unroll=4)

    for at, rows, is_left in ((0, 0, True), (1, 0, False), (2, 24, True), (3, 24, False)):
        cells = diff[rows : rows + 8, :]
        high = cells.astype(jnp.bfloat16).astype(jnp.float32)
        low = cells - high
        d = tab[POS, at]
        old = stage[d, 2, 8:16, :]
        if is_left:
            new = jnp.where((lane >= 4) & (lane < 8), pltpu.roll(high, 4, 1), old)
            new = jnp.where((lane >= 8) & (lane < 12), pltpu.roll(low, 8, 1), new)
        else:
            new = jnp.where((lane >= 120) & (lane < 124), pltpu.roll(high, 124, 1), old)
            new = jnp.where((lane >= 116) & (lane < 120), pltpu.roll(low, 120, 1), new)
        stage[d, 2, 8:16, :] = new

    def convert(q, carry):
        out[pl.ds(q * 8, 8)] = stage[pl.ds(q * 8, 8)].astype(jnp.bfloat16)
        return carry

    lax.fori_loop(0, OWNERS // 8, convert, 0)


def ocean_kernel(tab, recv, diff, above, below, before, after, out, onehot, dext, u0, u1):
    lane = lanes((8, 128))
    a_of, b_of = lane // 16, lane % 16
    K = OWNERS * 16
    own_in = recv[:, 0].reshape(K, 128)
    pair_in = recv[:, 1].reshape(K, 128)
    side_in = recv[:, 2].reshape(K, 128)

    pick_row = lax.broadcasted_iota(jnp.int32, (16, 128), 0)
    pick_lane = lanes((16, 128))
    label_lane = jnp.where(pick_row < 8, 36 + pick_row, 44 + pick_row)
    pick = ((label_lane == pick_lane) & (pick_row < 10)).astype(jnp.float32).astype(jnp.bfloat16)
    keys = lax.dot_general(pick, side_in, (((1,), (1,)), ((), ())), preferred_element_type=jnp.float32)
    early = pltpu.roll(keys, K - 8, 1)
    klane = lanes((8, K))
    sub = lax.broadcasted_iota(jnp.int32, (8, K), 0).astype(jnp.float32)
    late = (klane & 8) != 0

    def spread(rows, at):
        return jnp.broadcast_to(rows[at : at + 1, :], (8, K))

    def both(at):
        return jnp.where(late, spread(keys, at + 1), spread(early, at)) - sub

    def first(at):
        return jnp.where(late, -1000.0, spread(early, at)) - sub

    def hot(base, key, count):
        for t in range(0, count, 2):
            pair = [jnp.where(key == 8.0 * (t + q), 1.0, 0.0) for q in range(2)]
            onehot[pl.ds(base + t * 8, 16), :] = jnp.concatenate(pair, axis=0).astype(jnp.bfloat16)

    hot(0, both(0), 32)
    hot(256, both(2), 8)
    hot(320, both(4), 8)
    hot(384, first(6), 4)
    hot(416, first(7), 4)
    hot(448, first(8), 4)
    hot(480, first(9), 4)
    hot(512, jnp.where(late, (klane & 7).astype(jnp.float32), -1000.0) - sub, 2)

    def dot(lo, hi, rhs):
        return jnp.dot(onehot[lo:hi, :], rhs, preferred_element_type=jnp.float32)

    own = dot(0, 256, own_in)
    pairs = dot(256, 384, pair_in)
    sides = dot(384, 528, side_in)

    def tile(x, at):
        return x[at * 8 : at * 8 + 8, :]

    def put_side(cells, rows):
        for a, e in rows:
            right = pltpu.roll(cells, (128 - 16 * a) % 128, 1)
            left = pltpu.roll(cells, (112 - 16 * a) % 128, 1)
            u0[e, :, 128:256] = jnp.where(lane < 4, right, jnp.where(lane >= 124, left, 0.0))

    for tx in range(4):
        rows = swap_blocks([tile(own, tx * 8 + ty) for ty in range(8)])
        for a in range(8):
            u0[4 + tx * 8 + a, :, 0:128] = rows[a]
        r = tile(sides, tx) + pltpu.roll(tile(sides, 4 + tx), 124, 1)
        l = tile(sides, 8 + tx) + pltpu.roll(tile(sides, 12 + tx), 4, 1)
        put_side(jnp.where(b_of < 4, r, l), [(a, 4 + tx * 8 + a) for a in range(8)])
    rows = swap_blocks([tile(pairs, ty) for ty in range(8)])
    for a in range(4):
        u0[36 + a, :, 0:128] = rows[a]
    rows = swap_blocks([tile(pairs, 8 + ty) for ty in range(8)])
    for a in range(4, 8):
        u0[a - 4, :, 0:128] = rows[a]
    put_side(tile(sides, 16), [(a, 36 + a) for a in range(4)] + [(a, a - 4) for a in range(4, 8)])

    def flag(at):
        return tab[POS, at].astype(jnp.float32)

    def corner(at):
        s = tab[POS, at]
        z = recv[jnp.minimum(s, OWNERS - 1), 2].astype(jnp.float32)[8:16, :]
        z = jnp.where(s < OWNERS, z, 0.0)
        left = pltpu.roll(z, 4, 1) + pltpu.roll(z, 8, 1)
        right = pltpu.roll(z, 124, 1) + pltpu.roll(z, 120, 1)
        return left if at % 2 == 0 else right

    def ends(left, right):
        return jnp.where(lane < 4, right, jnp.where(lane >= 124, left, 0.0))

    dext[0:8, 0:128] = above[40:48, :] * flag(4)
    dext[40:48, 0:128] = below[16:24, :] * flag(5)
    dext[8:40, 0:128] = diff[...]
    dext[0:8, 128:256] = ends(corner(0), corner(1))
    dext[40:48, 128:256] = ends(corner(2), corner(3))
    for q in range(4):
        dext[8 + q * 8 : 16 + q * 8, 128:256] = ends(
            before[8 + q * 8 : 16 + q * 8, :] * flag(6), after[8 + q * 8 : 16 + q * 8, :] * flag(7)
        )

    src, dst = u0, u1
    for sweep in range(SWEEPS):
        for e in range(sweep + 1, 39 - sweep):
            u = src[e]
            beside = src[e + 1] + src[e - 1] + pltpu.roll(u, 255, 1) + pltpu.roll(u, 1, 1)
            d = jnp.broadcast_to(dext[e + 4 : e + 5, :], (8, 256))
            new = u + d * (beside - 4.0 * u)
            if sweep < SWEEPS - 1:
                dst[e] = new
            else:
                out[pl.ds(e - 4, 8, stride=OXD), :] = new[:, :128]
        src, dst = dst, src


def record_table(owner, source, target, weight):
    gx, gy = lax.axis_index("gx"), lax.axis_index("gy")
    me = gx * NGY + gy
    ids = jnp.arange(RECS, dtype=jnp.int32)
    earlier = (owner[:, None] == owner[None, :]) & (ids[None, :] < ids[:, None])
    slot = jnp.sum(earlier.astype(jnp.int32), axis=1)
    ox, oy = owner // NGY, owner % NGY
    tx, ty = target // 8, target % 8
    sx = jnp.where(tx == 0, -1, jnp.where(tx == 3, 1, 0))
    sy = jnp.where(ty == 0, -1, jnp.where(ty == 7, 1, 0))
    ok_x = (sx != 0) & (ox + sx >= 0) & (ox + sx < NGX)
    ok_y = (sy != 0) & (oy + sy >= 0) & (oy + sy < NGY)
    dx = jnp.where(ok_x, owner + sx * NGY, OWNERS)
    dy = jnp.where(ok_y, owner + sy, OWNERS)
    dc = jnp.where(ok_x & ok_y, owner + sx * NGY + sy, OWNERS)
    kx = (tx == 3).astype(jnp.int32)
    ky = (ty == 7).astype(jnp.int32)
    ti, tj = source // 16, source % 16
    t8 = (ti * 16 + (tj % 8) * 2 + tj // 8) * 8

    def near(du, dv):
        ok = (gx + du >= 0) & (gx + du < NGX) & (gy + dv >= 0) & (gy + dv < NGY)
        return jnp.where(ok, me + du * NGY + dv, OWNERS)

    at = ids
    flags = [near(-1, -1), near(-1, 1), near(1, -1), near(1, 1), gx > 0, gx < NGX - 1, gy > 0, gy < NGY - 1]
    pos = jnp.zeros((RECS,), jnp.int32)
    for n, value in enumerate(flags):
        pos = jnp.where(at == n, value.astype(jnp.int32), pos)
    rows = [
        weight, t8, owner, slot, dx, dy, dc, kx, 2 + ky * 2 + slot, 6 + kx * 2 + ky,
        jnp.where(ky == 0, 4 * slot, (128 - 4 * slot) % 128),
        36 + slot, 38 + 2 * kx + slot, jnp.where(ky == 0, 42, 52) + slot,
        target * 8, ty * 8, tx * 8, pos,
    ]
    return jnp.stack(rows)


def local(flux, diffusivity, remap_bank, rec_owner, rec_source, rec_target, rec_weight):
    tab = record_table(rec_owner, rec_source, rec_target, rec_weight)

    def gx_message(i):
        return jnp.concatenate([flux[:, i, :128], flux[:, i, 128:], diffusivity], axis=0)

    def gy_message(j):
        return jnp.concatenate([jnp.pad(flux[:, :, j], ((0, 0), (0, 64))), diffusivity], axis=0)

    def shift(x, axis, count, by):
        return lax.ppermute(x, axis, [(i, (i + by) % count) for i in range(count)])

    above = shift(gx_message(AXD - 1), "gx", NGX, 1)
    below = shift(gx_message(0), "gx", NGX, -1)
    before = shift(gy_message(AYD - 1), "gy", NGY, 1)
    after = shift(gy_message(0), "gy", NGY, -1)

    vmem = pl.BlockSpec(memory_space=pltpu.VMEM)
    smem = pl.BlockSpec(memory_space=pltpu.SMEM)
    outgoing = pl.pallas_call(
        send_kernel,
        out_shape=jax.ShapeDtypeStruct((OWNERS, 3, 16, 128), jnp.bfloat16),
        in_specs=[smem, pl.BlockSpec(memory_space=pl.ANY)] + [vmem] * 6,
        out_specs=vmem,
        scratch_shapes=[
            pltpu.VMEM((512, 768), jnp.bfloat16),
            pltpu.VMEM((NWB, 512, 128), jnp.float32),
            pltpu.VMEM((OWNERS + 1, 3, 16, 128), jnp.float32),
            pltpu.VMEM((10, 8, 128), jnp.float32),
            pltpu.VMEM((2, F * AXD, 128), jnp.float32),
            pltpu.SemaphoreType.DMA((2,)),
        ],
        name="remap_send",
    )(tab, flux.reshape(F * AXD, AYD), above, below, before, after, diffusivity, remap_bank.reshape(NWB, 768, 128))
    arrived = lax.all_to_all(outgoing, ("gx", "gy"), split_axis=0, concat_axis=0, tiled=True)
    ocean = pl.pallas_call(
        ocean_kernel,
        out_shape=jax.ShapeDtypeStruct((F * OXD, OYD), jnp.float32),
        in_specs=[smem] + [vmem] * 6,
        out_specs=vmem,
        scratch_shapes=[
            pltpu.VMEM((528, OWNERS * 16), jnp.bfloat16),
            pltpu.VMEM((48, 256), jnp.float32),
            pltpu.VMEM((40, 8, 256), jnp.float32),
            pltpu.VMEM((40, 8, 256), jnp.float32),
        ],
        name="ocean",
    )(tab, arrived, diffusivity, above, below, before, after)
    return ocean.reshape(F, OXD, OYD)


def solution(mesh):
    in_specs = (
        P(None, "gx", "gy"),
        P("gx", "gy"),
        P(),
        P(("gx", "gy")),
        P(("gx", "gy")),
        P(("gx", "gy")),
        P(("gx", "gy")),
    )
    return jax.shard_map(local, mesh=mesh, in_specs=in_specs, out_specs=P(None, "gx", "gy"), check_vma=False)
```

```python
import jax
import jax.numpy as jnp
from jax import lax
from jax.experimental import pallas as pl
from jax.experimental.pallas import tpu as pltpu
from jax.sharding import PartitionSpec as P

F = 8
AXD, AYD = 64, 256
OXD, OYD = 32, 128
NWB = 16
RECS = 128
SWEEPS = 4
OWNERS = 128
NGX, NGY = 8, 16
(PROD, OWN, XROW, YROW, CROW, KX, YQ, CC, SHIFT, OWNER, XTO, YTO, PO, PX, PY, VO, VX, VY) = range(18)
TAB_ROWS = 24
ABSENT = 256.0
CORNERS = ((-1, -1), (-1, 1), (1, -1), (1, 1))


def lanes(shape):
    return lax.broadcasted_iota(jnp.int32, shape, 1)


def swap_blocks(v):
    block = lanes((8, 128)) // 16
    for s in range(3):
        d = 1 << s
        high = (block & d) != 0
        n = list(v)
        for p in range(8):
            if not p & d:
                a, b = v[p], v[p | d]
                n[p] = jnp.where(high, pltpu.roll(b, 16 * d, 1), a)
                n[p | d] = jnp.where(high, b, pltpu.roll(a, 128 - 16 * d, 1))
        v = n
    return v


def load_flux(flux_in, flux, sems):
    return [pltpu.make_async_copy(flux_in.at[:, pl.ds(g * 128, 128)], flux.at[g], sems.at[g]) for g in range(2)]


def neighbour(du, dv):
    gx, gy = lax.axis_index("gx") + du, lax.axis_index("gy") + dv
    return jnp.where((gx >= 0) & (gx < NGX) & (gy >= 0) & (gy < NGY), gx * NGY + gy, OWNERS)


def prepare_kernel(flux_in, diff, owner_in, source_in, target_in, weight_in, down, up, after, before, tab, flux, sems):
    copies = load_flux(flux_in, flux, sems)
    for copy in copies:
        copy.start()
    lane = lanes((8, 128))
    owner, source, target, weight = owner_in[...], source_in[...], target_in[...], weight_in[...]
    across = jnp.broadcast_to(owner, (RECS, RECS))
    along = jnp.transpose(across.astype(jnp.float32)).astype(jnp.int32)
    sub = lax.broadcasted_iota(jnp.int32, (RECS, RECS), 0)
    earlier = jnp.where((across == along) & (sub < lanes((RECS, RECS))), 1.0, 0.0)
    slot = jnp.sum(earlier, axis=0, keepdims=True).astype(jnp.int32)
    ox, oy = owner >> 4, owner & 15
    tx, ty = target >> 3, target & 7
    sx = jnp.where(tx == 0, -1, jnp.where(tx == 3, 1, 0))
    sy = jnp.where(ty == 0, -1, jnp.where(ty == 7, 1, 0))
    ok_x = (sx != 0) & (ox + sx >= 0) & (ox + sx < NGX)
    ok_y = (sy != 0) & (oy + sy >= 0) & (oy + sy < NGY)
    dx = jnp.where(ok_x, owner + sx * NGY, OWNERS)
    dy = jnp.where(ok_y, owner + sy, OWNERS)
    dc = jnp.where(ok_x & ok_y, owner + sx * NGY + sy, OWNERS)
    kx = jnp.where(tx == 3, 1, 0)
    ky = jnp.where(ty == 7, 1, 0)
    ti, tj = source >> 4, source & 15
    t8 = (ti * 16 + (tj & 7) * 2 + (tj >> 3)) * 8
    rows = [
        weight * 512 + t8, owner * 16 + slot * 8, dx * 16 + slot * 8, dy * 8, dc * 16 + slot * 8,
        kx, jnp.where(ky == 0, slot, 3 - slot), kx * 4 + ky * 3, jnp.where(ky == 0, 4 * slot, (128 - 4 * slot) & 127),
        owner, dx, dy, 36 + slot, 38 + 2 * kx + slot, jnp.where(ky == 0, 42, 52) + slot,
        target * 8 + 1, ty * 8 + 1, tx * 8 + 1,
    ]
    for n, value in enumerate(rows):
        tab[n : n + 1, :] = value
    for n in range(len(rows), TAB_ROWS):
        tab[n : n + 1, :] = slot

    for to in (down, up):
        to[16:48, :] = diff[...]
    for to in (after, before):
        to[8:40, :] = diff[...]
    for copy in copies:
        copy.wait()

    def row(i, g):
        return flux[g, pl.ds(i, 8, stride=AXD), :]

    for g in range(2):
        down[g * 8 : g * 8 + 8, :] = row(AXD - 1, g)
        up[g * 8 : g * 8 + 8, :] = row(0, g)
    last = jnp.zeros((8, 128), jnp.float32)
    first = jnp.zeros((8, 128), jnp.float32)
    for i in range(AXD):
        last = jnp.where(lane == i, row(i, 1)[:, 127:128], last)
        first = jnp.where(lane == i, row(i, 0)[:, 0:1], first)
    after[0:8, :] = last
    before[0:8, :] = first


def send_kernel(tab, tabv, flux_in, above, below, before, after, diff, bank, out, lhs, prod, owns, pairs, sides, corners, lab, flux, sems):
    copies = load_flux(flux_in, flux, sems)
    for copy in copies:
        copy.start()
    lane = lanes((8, 128))
    sub = lax.broadcasted_iota(jnp.int32, (8, 128), 0)
    a_of, b_of = lane // 16, lane % 16

    rows3 = lax.broadcasted_iota(jnp.int32, (128, 3 * RECS), 0)

    def three(*at):
        return jnp.concatenate([jnp.broadcast_to(tabv[n : n + 1, :], (128, RECS)) for n in at], axis=1)

    going = jnp.where(three(OWNER, XTO, YTO) == rows3, 1.0, 0.0).astype(jnp.bfloat16)
    label = jnp.where(three(PO, PX, PY) == rows3, three(VO, VX, VY), 0).astype(jnp.float32).astype(jnp.bfloat16)
    lab[...] = lax.dot_general(going, label, (((1,), (1,)), ((), ())), preferred_element_type=jnp.float32)
    is_label = (a_of == 2) & (b_of >= 4) & (b_of < 12) | (a_of == 3) & (b_of >= 4) & (b_of < 6)
    absent = jnp.where(is_label, ABSENT, 0.0)
    offset = (sub - 1).astype(jnp.float32)

    zero = jnp.zeros((8, 128), jnp.float32)

    def clear(o, carry):
        at = pl.multiple_of(o * 16, 16)
        half = pl.multiple_of(o * 8, 8)
        owns[pl.ds(at, 8), :] = zero
        owns[pl.ds(at + 8, 8), :] = zero
        pairs[pl.ds(at, 8), :] = zero
        pairs[pl.ds(at + 8, 8), :] = zero
        sides[pl.ds(half, 8), :] = zero
        corners[pl.ds(at, 8), :] = zero
        corners[pl.ds(at + 8, 8), :] = zero
        return carry

    lax.fori_loop(0, OWNERS, clear, 0, unroll=4)

    wide = lanes((8, 256))
    left, right = before[0:8, :], after[0:8, :]

    def row(i):
        if i < 0:
            return jnp.concatenate([above[0:8, :], above[8:16, :]], axis=1)
        if i >= AXD:
            return jnp.concatenate([below[0:8, :], below[8:16, :]], axis=1)
        return jnp.concatenate([flux[g, pl.ds(i, 8, stride=AXD), :] for g in range(2)], axis=1)

    for copy in copies:
        copy.wait()
    for ti in range(4):
        x = [row(i) for i in range(ti * 16 - 1, ti * 16 + 17)]
        for k in range(3):
            vals = []
            for a in range(16):
                i = ti * 16 + a
                if k == 0:
                    vals.append(x[a + 1])
                elif k == 1:
                    vals.append((x[a + 2] - x[a]) * 0.5)
                else:
                    nxt = jnp.where(wide == 255, right[:, i : i + 1], pltpu.roll(x[a + 1], 255, 1))
                    prv = jnp.where(wide == 0, left[:, i : i + 1], pltpu.roll(x[a + 1], 1, 1))
                    vals.append((nxt - prv) * 0.5)
            for h in range(2):
                y = [swap_blocks([vals[h * 8 + q][:, g * 128 : (g + 1) * 128] for q in range(8)]) for g in range(2)]
                for q in range(8):
                    lhs[pl.ds((ti * 8 + q) * 16, 16), pl.ds(k * 256 + h * 128, 128)] = jnp.concatenate(
                        [y[0][q], y[1][q]], axis=0
                    ).astype(jnp.bfloat16)

    def product(n, carry):
        rhs = jnp.concatenate([bank[2 * n], bank[2 * n + 1]], axis=1)
        res = jnp.dot(lhs[...], rhs, preferred_element_type=jnp.float32)
        at = pl.multiple_of(n * 1024, 1024)
        prod[pl.ds(at, 512), :] = res[:, :128]
        prod[pl.ds(at + 512, 512), :] = res[:, 128:]
        return carry

    lax.fori_loop(0, NWB // 2, product, 0)

    half_of, quarter_of = lane // 64, b_of // 4
    code = half_of * 4 + quarter_of

    def rows(ref, at):
        return ref.at[pl.ds(pl.multiple_of(at, 8), 8), :]

    for r in range(RECS):
        value = rows(prod, tab[PROD, r])[...]
        rows(owns, tab[OWN, r])[...] = value
        pltpu.store(rows(pairs, tab[XROW, r]), value, mask=half_of == tab[KX, r])
        pltpu.store(rows(sides, tab[YROW, r]), pltpu.roll(value, tab[SHIFT, r], 1), mask=quarter_of == tab[YQ, r])
        pltpu.store(rows(corners, tab[CROW, r]), value, mask=code == tab[CC, r])

    for du, dv in CORNERS:
        first = 0 if du < 0 else 24
        cells = diff[first : first + 8, :]
        high = cells.astype(jnp.bfloat16).astype(jnp.float32)
        low = cells - high
        to = rows(corners, neighbour(du, dv) * 16)
        if dv < 0:
            pltpu.store(to, pltpu.roll(high, 4, 1), mask=(lane >= 4) & (lane < 8))
            pltpu.store(to, pltpu.roll(low, 8, 1), mask=(lane >= 8) & (lane < 12))
        else:
            pltpu.store(to, pltpu.roll(high, 124, 1), mask=(lane >= 120) & (lane < 124))
            pltpu.store(to, pltpu.roll(low, 120, 1), mask=(lane >= 116) & (lane < 120))

    def convert(o, carry):
        at = pl.multiple_of(o * 16, 16)
        half = pl.ds(pl.multiple_of(o * 8, 8), 8)
        found = jnp.broadcast_to(lab[pl.ds(o, 1), :], (8, 128))
        tags = jnp.where(found > 0, found + offset, absent)
        last = tags + (corners[pl.ds(at, 8), :] + corners[pl.ds(at + 8, 8), :])
        out[o, 0] = owns[pl.ds(at, 16), :].astype(jnp.bfloat16)
        out[o, 1] = pairs[pl.ds(at, 16), :].astype(jnp.bfloat16)
        out[o, 2] = jnp.concatenate([sides[half, :], last], axis=0).astype(jnp.bfloat16)
        return carry

    lax.fori_loop(0, OWNERS, convert, 0, unroll=8)


def ocean_kernel(recv, diff, above, below, before, after, out, onehot, dext, u0, u1):
    lane = lanes((8, 128))
    a_of, b_of = lane // 16, lane % 16
    K = OWNERS * 16
    own_in = recv[:, 0].reshape(K, 128)
    pair_in = recv[:, 1].reshape(K, 128)
    side_in = recv[:, 2].reshape(K, 128)

    pick_row = lax.broadcasted_iota(jnp.int32, (16, 128), 0)
    pick_lane = lanes((16, 128))
    label_lane = jnp.where(pick_row < 8, 36 + pick_row, 44 + pick_row)
    pick = ((label_lane == pick_lane) & (pick_row < 10)).astype(jnp.float32).astype(jnp.bfloat16)
    keys = lax.dot_general(pick, side_in, (((1,), (1,)), ((), ())), preferred_element_type=jnp.float32)
    early = pltpu.roll(keys, K - 8, 1)
    klane = lanes((8, K))
    sub = lax.broadcasted_iota(jnp.int32, (8, K), 0).astype(jnp.float32)
    late = (klane & 8) != 0

    def spread(rows, at):
        return jnp.broadcast_to(rows[at : at + 1, :], (8, K))

    def both(at):
        return jnp.where(late, spread(keys, at + 1), spread(early, at)) - sub

    def first(at):
        return jnp.where(late, -1000.0, spread(early, at)) - sub

    def hot(base, key, count):
        for t in range(0, count, 2):
            pair = [jnp.where(key == 8.0 * (t + q), 1.0, 0.0) for q in range(2)]
            onehot[pl.ds(base + t * 8, 16), :] = jnp.concatenate(pair, axis=0).astype(jnp.bfloat16)

    hot(0, both(0), 32)
    hot(256, both(2), 8)
    hot(320, both(4), 8)
    hot(384, first(6), 4)
    hot(416, first(7), 4)
    hot(448, first(8), 4)
    hot(480, first(9), 4)
    hot(512, jnp.where(late, (klane & 7).astype(jnp.float32), -1000.0) - sub, 2)

    def dot(lo, hi, rhs):
        return jnp.dot(onehot[lo:hi, :], rhs, preferred_element_type=jnp.float32)

    own = dot(0, 256, own_in)
    pairs = dot(256, 384, pair_in)
    sides = dot(384, 528, side_in)

    def tile(x, at):
        return x[at * 8 : at * 8 + 8, :]

    def put_side(cells, rows):
        for a, e in rows:
            right = pltpu.roll(cells, (128 - 16 * a) % 128, 1)
            left = pltpu.roll(cells, (112 - 16 * a) % 128, 1)
            u0[e, :, 128:256] = jnp.where(lane < 4, right, jnp.where(lane >= 124, left, 0.0))

    for tx in range(4):
        rows = swap_blocks([tile(own, tx * 8 + ty) for ty in range(8)])
        for a in range(8):
            u0[4 + tx * 8 + a, :, 0:128] = rows[a]
        r = tile(sides, tx) + pltpu.roll(tile(sides, 4 + tx), 124, 1)
        l = tile(sides, 8 + tx) + pltpu.roll(tile(sides, 12 + tx), 4, 1)
        put_side(jnp.where(b_of < 4, r, l), [(a, 4 + tx * 8 + a) for a in range(8)])
    rows = swap_blocks([tile(pairs, ty) for ty in range(8)])
    for a in range(4):
        u0[36 + a, :, 0:128] = rows[a]
    rows = swap_blocks([tile(pairs, 8 + ty) for ty in range(8)])
    for a in range(4, 8):
        u0[a - 4, :, 0:128] = rows[a]
    put_side(tile(sides, 16), [(a, 36 + a) for a in range(4)] + [(a, a - 4) for a in range(4, 8)])

    def flag(du, dv):
        return jnp.where(neighbour(du, dv) < OWNERS, 1.0, 0.0)

    def corner(du, dv):
        s = neighbour(du, dv)
        z = recv[jnp.minimum(s, OWNERS - 1), 2].astype(jnp.float32)[8:16, :]
        z = jnp.where(s < OWNERS, z, 0.0)
        left = pltpu.roll(z, 4, 1) + pltpu.roll(z, 8, 1)
        right = pltpu.roll(z, 124, 1) + pltpu.roll(z, 120, 1)
        return left if dv < 0 else right

    def ends(left, right):
        return jnp.where(lane < 4, right, jnp.where(lane >= 124, left, 0.0))

    dext[0:8, 0:128] = above[40:48, :] * flag(-1, 0)
    dext[40:48, 0:128] = below[16:24, :] * flag(1, 0)
    dext[8:40, 0:128] = diff[...]
    dext[0:8, 128:256] = ends(corner(-1, -1), corner(-1, 1))
    dext[40:48, 128:256] = ends(corner(1, -1), corner(1, 1))
    for q in range(4):
        dext[8 + q * 8 : 16 + q * 8, 128:256] = ends(
            before[8 + q * 8 : 16 + q * 8, :] * flag(0, -1), after[8 + q * 8 : 16 + q * 8, :] * flag(0, 1)
        )

    src, dst = u0, u1
    for sweep in range(SWEEPS):
        for e in range(sweep + 1, 39 - sweep):
            u = src[e]
            beside = src[e + 1] + src[e - 1] + pltpu.roll(u, 255, 1) + pltpu.roll(u, 1, 1)
            d = jnp.broadcast_to(dext[e + 4 : e + 5, :], (8, 256))
            new = u + d * (beside - 4.0 * u)
            if sweep < SWEEPS - 1:
                dst[e] = new
            else:
                out[pl.ds(e - 4, 8, stride=OXD), :] = new[:, :128]
        src, dst = dst, src


def local(flux, diffusivity, remap_bank, rec_owner, rec_source, rec_target, rec_weight):
    vmem = pl.BlockSpec(memory_space=pltpu.VMEM)
    smem = pl.BlockSpec(memory_space=pltpu.SMEM)
    anywhere = pl.BlockSpec(memory_space=pl.ANY)
    flux_rows = flux.reshape(F * AXD, AYD)
    flux_scratch = [pltpu.VMEM((2, F * AXD, 128), jnp.float32), pltpu.SemaphoreType.DMA((2,))]
    records = [x.reshape(1, RECS) for x in (rec_owner, rec_source, rec_target, rec_weight)]
    f32, i32 = jnp.float32, jnp.int32
    down, up, right, left, tab = pl.pallas_call(
        prepare_kernel,
        out_shape=[jax.ShapeDtypeStruct((48, 128), f32)] * 2
        + [jax.ShapeDtypeStruct((40, 128), f32)] * 2
        + [jax.ShapeDtypeStruct((TAB_ROWS, RECS), i32)],
        in_specs=[anywhere] + [vmem] * 5,
        out_specs=[vmem] * 5,
        scratch_shapes=flux_scratch,
        name="prepare",
    )(flux_rows, diffusivity, *records)

    def shift(x, axis, count, by):
        return lax.ppermute(x, axis, [(i, (i + by) % count) for i in range(count)])

    above = shift(down, "gx", NGX, 1)
    below = shift(up, "gx", NGX, -1)
    before = shift(right, "gy", NGY, 1)
    after = shift(left, "gy", NGY, -1)

    outgoing = pl.pallas_call(
        send_kernel,
        out_shape=jax.ShapeDtypeStruct((OWNERS, 3, 16, 128), jnp.bfloat16),
        in_specs=[smem, vmem, anywhere] + [vmem] * 6,
        out_specs=vmem,
        scratch_shapes=[
            pltpu.VMEM((512, 768), jnp.bfloat16),
            pltpu.VMEM((NWB * 512, 128), f32),
            pltpu.VMEM((OWNERS * 16, 128), f32),
            pltpu.VMEM((OWNERS * 16 + 16, 128), f32),
            pltpu.VMEM((OWNERS * 8 + 8, 128), f32),
            pltpu.VMEM((OWNERS * 16 + 16, 128), f32),
            pltpu.VMEM((OWNERS, 128), f32),
        ]
        + flux_scratch,
        name="remap_send",
    )(tab, tab, flux_rows, above, below, before, after, diffusivity, remap_bank.reshape(NWB, 768, 128))
    arrived = lax.all_to_all(outgoing, ("gx", "gy"), split_axis=0, concat_axis=0, tiled=True)
    ocean = pl.pallas_call(
        ocean_kernel,
        out_shape=jax.ShapeDtypeStruct((F * OXD, OYD), f32),
        in_specs=[vmem] * 6,
        out_specs=vmem,
        scratch_shapes=[
            pltpu.VMEM((528, OWNERS * 16), jnp.bfloat16),
            pltpu.VMEM((48, 256), f32),
            pltpu.VMEM((40, 8, 256), f32),
            pltpu.VMEM((40, 8, 256), f32),
        ],
        name="ocean",
    )(arrived, diffusivity, above, below, before, after)
    return ocean.reshape(F, OXD, OYD)


def solution(mesh):
    in_specs = (
        P(None, "gx", "gy"),
        P("gx", "gy"),
        P(),
        P(("gx", "gy")),
        P(("gx", "gy")),
        P(("gx", "gy")),
        P(("gx", "gy")),
    )
    return jax.shard_map(local, mesh=mesh, in_specs=in_specs, out_specs=P(None, "gx", "gy"), check_vma=False)
```

```python
import jax
import jax.numpy as jnp
from jax import lax
from jax.experimental import pallas as pl
from jax.experimental.pallas import tpu as pltpu
from jax.sharding import PartitionSpec as P


F = 8
AXD, AYD = 64, 256
OXD, OYD = 32, 128
NWB = 16
RECS = 128
SWEEPS = 4
OWNERS = 128
NGX, NGY = 8, 16
(PROD, OWN, XROW, YROW, CROW, KX, YQ, CC, SHIFT, OWNER, XTO, YTO, PO, PX, PY, VO, VX, VY) = range(18)
TAB_ROWS = 24
ABSENT = 256.0
CORNERS = ((-1, -1), (-1, 1), (1, -1), (1, 1))


def lanes(shape):
    return lax.broadcasted_iota(jnp.int32, shape, 1)


def swap_blocks(v):
    block = lanes(v[0].shape) // 16
    for s in range(3):
        d = 1 << s
        high = (block & d) != 0
        n = list(v)
        for p in range(8):
            if not p & d:
                a, b = v[p], v[p | d]
                if d == 4:
                    up = down = pltpu.roll(jnp.where(high, a, b), 64, 1)
                else:
                    up, down = pltpu.roll(b, 16 * d, 1), pltpu.roll(a, 128 - 16 * d, 1)
                n[p] = jnp.where(high, up, a)
                n[p | d] = jnp.where(high, b, down)
        v = n
    return v


def load_flux(flux_in, flux, sems):
    return [pltpu.make_async_copy(flux_in.at[:, pl.ds(g * 128, 128)], flux.at[g], sems.at[g]) for g in range(2)]


def neighbour(du, dv):
    gx, gy = lax.axis_index("gx") + du, lax.axis_index("gy") + dv
    return jnp.where((gx >= 0) & (gx < NGX) & (gy >= 0) & (gy < NGY), gx * NGY + gy, OWNERS)


def even(axis):
    return lax.axis_index(axis) % 2 == 0


def sides_of(from_c, from_x, from_a, from_b):
    even_x, even_y = even("gx"), even("gy")
    return (
        lambda lo, hi: jnp.where(even_x, from_x[lo:hi, :], from_c[lo:hi, :]),
        lambda lo, hi: jnp.where(even_x, from_c[lo:hi, :], from_x[lo:hi, :]),
        lambda lo, hi: jnp.where(even_y, from_b[lo:hi, :], from_a[lo:hi, :]),
        lambda lo, hi: jnp.where(even_y, from_a[lo:hi, :], from_b[lo:hi, :]),
    )


def prepare_kernel(flux_in, diff, owner_in, source_in, target_in, weight_in, to_c, to_x, to_a, to_b, tab, flux, sems):
    copies = load_flux(flux_in, flux, sems)
    for copy in copies:
        copy.start()
    lane = lanes((8, 128))
    owner, source, target, weight = owner_in[...], source_in[...], target_in[...], weight_in[...]
    across = jnp.broadcast_to(owner, (RECS, RECS))
    along = jnp.transpose(across.astype(jnp.float32)).astype(jnp.int32)
    sub = lax.broadcasted_iota(jnp.int32, (RECS, RECS), 0)
    earlier = jnp.where((across == along) & (sub < lanes((RECS, RECS))), 1.0, 0.0)
    slot = jnp.sum(earlier, axis=0, keepdims=True).astype(jnp.int32)
    ox, oy = owner >> 4, owner & 15
    tx, ty = target >> 3, target & 7
    sx = jnp.where(tx == 0, -1, jnp.where(tx == 3, 1, 0))
    sy = jnp.where(ty == 0, -1, jnp.where(ty == 7, 1, 0))
    ok_x = (sx != 0) & (ox + sx >= 0) & (ox + sx < NGX)
    ok_y = (sy != 0) & (oy + sy >= 0) & (oy + sy < NGY)
    dx = jnp.where(ok_x, owner + sx * NGY, OWNERS)
    dy = jnp.where(ok_y, owner + sy, OWNERS)
    dc = jnp.where(ok_x & ok_y, owner + sx * NGY + sy, OWNERS)
    kx = jnp.where(tx == 3, 1, 0)
    ky = jnp.where(ty == 7, 1, 0)
    ti, tj = source >> 4, source & 15
    t8 = (ti * 16 + (tj & 7) * 2 + (tj >> 3)) * 8
    rows = [
        weight * 512 + t8, owner * 16 + slot * 8, dx * 16 + slot * 8, dy * 8, dc * 16 + slot * 8,
        kx, jnp.where(ky == 0, slot, 3 - slot), kx * 4 + ky * 3, jnp.where(ky == 0, 4 * slot, (128 - 4 * slot) & 127),
        owner, dx, dy, 36 + slot, 38 + 2 * kx + slot, jnp.where(ky == 0, 42, 52) + slot,
        target * 8 + 1, ty * 8 + 1, tx * 8 + 1,
    ]
    for n, value in enumerate(rows):
        tab[n : n + 1, :] = value
    for n in range(len(rows), TAB_ROWS):
        tab[n : n + 1, :] = slot

    for to in (to_c, to_x):
        to[16:48, :] = diff[...]
    for to in (to_a, to_b):
        to[8:40, :] = diff[...]
    for copy in copies:
        copy.wait()

    def row(i, g):
        return flux[g, pl.ds(i, 8, stride=AXD), :]

    even_x, even_y = even("gx"), even("gy")
    for g in range(2):
        bottom, top = row(AXD - 1, g), row(0, g)
        to_c[g * 8 : g * 8 + 8, :] = jnp.where(even_x, bottom, top)
        to_x[g * 8 : g * 8 + 8, :] = jnp.where(even_x, top, bottom)
    last = jnp.zeros((8, 128), jnp.float32)
    first = jnp.zeros((8, 128), jnp.float32)
    for i in range(AXD):
        last = jnp.where(lane == i, row(i, 1)[:, 127:128], last)
        first = jnp.where(lane == i, row(i, 0)[:, 0:1], first)
    to_a[0:8, :] = jnp.where(even_y, last, first)
    to_b[0:8, :] = jnp.where(even_y, first, last)


def send_kernel(tab, tabv, flux_in, from_c, from_x, from_a, from_b, diff, bank, out, lhs, prod, owns, pairs, sides, corners, lab, flux, sems):
    copies = load_flux(flux_in, flux, sems)
    for copy in copies:
        copy.start()
    lane = lanes((8, 128))
    sub = lax.broadcasted_iota(jnp.int32, (8, 128), 0)
    a_of, b_of = lane // 16, lane % 16

    rows3 = lax.broadcasted_iota(jnp.int32, (128, 3 * RECS), 0)

    def three(*at):
        return jnp.concatenate([jnp.broadcast_to(tabv[n : n + 1, :], (128, RECS)) for n in at], axis=1)

    going = jnp.where(three(OWNER, XTO, YTO) == rows3, 1.0, 0.0).astype(jnp.bfloat16)
    label = jnp.where(three(PO, PX, PY) == rows3, three(VO, VX, VY), 0).astype(jnp.float32).astype(jnp.bfloat16)
    lab[...] = lax.dot_general(going, label, (((1,), (1,)), ((), ())), preferred_element_type=jnp.float32)
    is_label = (a_of == 2) & (b_of >= 4) & (b_of < 12) | (a_of == 3) & (b_of >= 4) & (b_of < 6)
    absent = jnp.where(is_label, ABSENT, 0.0)
    offset = (sub - 1).astype(jnp.float32)

    zero = jnp.zeros((8, 128), jnp.float32)

    def clear(o, carry):
        at = pl.multiple_of(o * 16, 16)
        half = pl.multiple_of(o * 8, 8)
        owns[pl.ds(at, 8), :] = zero
        owns[pl.ds(at + 8, 8), :] = zero
        pairs[pl.ds(at, 8), :] = zero
        pairs[pl.ds(at + 8, 8), :] = zero
        sides[pl.ds(half, 8), :] = zero
        corners[pl.ds(at, 8), :] = zero
        corners[pl.ds(at + 8, 8), :] = zero
        return carry

    lax.fori_loop(0, OWNERS, clear, 0, unroll=4)

    wide = lanes((8, 256))
    above, below, before, after = sides_of(from_c, from_x, from_a, from_b)
    left, right = before(0, 8), after(0, 8)
    top = jnp.concatenate([above(0, 8), above(8, 16)], axis=1)
    bottom = jnp.concatenate([below(0, 8), below(8, 16)], axis=1)

    def row(i):
        if i < 0:
            return top
        if i >= AXD:
            return bottom
        return jnp.concatenate([flux[g, pl.ds(i, 8, stride=AXD), :] for g in range(2)], axis=1)

    for copy in copies:
        copy.wait()
    for ti in range(4):
        x = [row(i) for i in range(ti * 16 - 1, ti * 16 + 17)]
        for k in range(3):
            vals = []
            for a in range(16):
                i = ti * 16 + a
                if k == 0:
                    vals.append(x[a + 1])
                elif k == 1:
                    vals.append((x[a + 2] - x[a]) * 0.5)
                else:
                    nxt = jnp.where(wide == 255, right[:, i : i + 1], pltpu.roll(x[a + 1], 255, 1))
                    prv = jnp.where(wide == 0, left[:, i : i + 1], pltpu.roll(x[a + 1], 1, 1))
                    vals.append((nxt - prv) * 0.5)
            for h in range(2):
                packed = [
                    jnp.concatenate([vals[h * 8 + q][:, :128], vals[h * 8 + q][:, 128:]], axis=0).astype(jnp.bfloat16)
                    for q in range(8)
                ]
                for q, tile in enumerate(swap_blocks(packed)):
                    lhs[pl.ds((ti * 8 + q) * 16, 16), pl.ds(k * 256 + h * 128, 128)] = tile

    def product(n, carry):
        rhs = jnp.concatenate([bank[2 * n], bank[2 * n + 1]], axis=1)
        res = jnp.dot(lhs[...], rhs, preferred_element_type=jnp.float32)
        at = pl.multiple_of(n * 1024, 1024)
        prod[pl.ds(at, 512), :] = res[:, :128]
        prod[pl.ds(at + 512, 512), :] = res[:, 128:]
        return carry

    lax.fori_loop(0, NWB // 2, product, 0)

    half_of, quarter_of = lane // 64, b_of // 4
    code = half_of * 4 + quarter_of

    def rows(ref, at):
        return ref.at[pl.ds(pl.multiple_of(at, 8), 8), :]

    for r in range(RECS):
        value = rows(prod, tab[PROD, r])[...]
        rows(owns, tab[OWN, r])[...] = value
        pltpu.store(rows(pairs, tab[XROW, r]), value, mask=half_of == tab[KX, r])
        pltpu.store(rows(sides, tab[YROW, r]), pltpu.roll(value, tab[SHIFT, r], 1), mask=quarter_of == tab[YQ, r])
        pltpu.store(rows(corners, tab[CROW, r]), value, mask=code == tab[CC, r])

    for du, dv in CORNERS:
        first = 0 if du < 0 else 24
        cells = diff[first : first + 8, :]
        high = cells.astype(jnp.bfloat16).astype(jnp.float32)
        low = cells - high
        to = rows(corners, neighbour(du, dv) * 16)
        if dv < 0:
            pltpu.store(to, pltpu.roll(high, 4, 1), mask=(lane >= 4) & (lane < 8))
            pltpu.store(to, pltpu.roll(low, 8, 1), mask=(lane >= 8) & (lane < 12))
        else:
            pltpu.store(to, pltpu.roll(high, 124, 1), mask=(lane >= 120) & (lane < 124))
            pltpu.store(to, pltpu.roll(low, 120, 1), mask=(lane >= 116) & (lane < 120))

    def convert(o, carry):
        at = pl.multiple_of(o * 16, 16)
        half = pl.ds(pl.multiple_of(o * 8, 8), 8)
        found = jnp.broadcast_to(lab[pl.ds(o, 1), :], (8, 128))
        tags = jnp.where(found > 0, found + offset, absent)
        last = tags + (corners[pl.ds(at, 8), :] + corners[pl.ds(at + 8, 8), :])
        out[o, 0] = owns[pl.ds(at, 16), :].astype(jnp.bfloat16)
        out[o, 1] = pairs[pl.ds(at, 16), :].astype(jnp.bfloat16)
        out[o, 2] = jnp.concatenate([sides[half, :], last], axis=0).astype(jnp.bfloat16)
        return carry

    lax.fori_loop(0, OWNERS, convert, 0, unroll=8)


def ocean_kernel(recv, diff, from_c, from_x, from_a, from_b, out, onehot, dext, u0, u1):
    lane = lanes((8, 128))
    b_of = lane % 16
    K = OWNERS * 16
    own_in = recv[:, 0].reshape(K, 128)
    pair_in = recv[:, 1].reshape(K, 128)
    side_in = recv[:, 2].reshape(K, 128)

    pick_row = lax.broadcasted_iota(jnp.int32, (16, 128), 0)
    pick_lane = lanes((16, 128))
    label_lane = jnp.where(pick_row < 8, 36 + pick_row, 44 + pick_row)
    pick = ((label_lane == pick_lane) & (pick_row < 10)).astype(jnp.float32).astype(jnp.bfloat16)
    keys = lax.dot_general(pick, side_in, (((1,), (1,)), ((), ())), preferred_element_type=jnp.float32)
    early = pltpu.roll(keys, K - 8, 1)
    klane = lanes((8, K))
    sub = lax.broadcasted_iota(jnp.int32, (8, K), 0).astype(jnp.float32)
    late = (klane & 8) != 0

    def spread(rows, at):
        return jnp.broadcast_to(rows[at : at + 1, :], (8, K))

    def both(at):
        return jnp.where(late, spread(keys, at + 1), spread(early, at)) - sub

    def first(at):
        return jnp.where(late, -1000.0, spread(early, at)) - sub

    def hot(base, key, count):
        for t in range(0, count, 2):
            pair = [jnp.where(key == 8.0 * (t + q), 1.0, 0.0) for q in range(2)]
            onehot[pl.ds(base + t * 8, 16), :] = jnp.concatenate(pair, axis=0).astype(jnp.bfloat16)

    hot(0, both(0), 32)
    hot(256, both(2), 8)
    hot(320, both(4), 8)
    hot(384, first(6), 4)
    hot(416, first(7), 4)
    hot(448, first(8), 4)
    hot(480, first(9), 4)
    hot(512, jnp.where(late, (klane & 7).astype(jnp.float32), -1000.0) - sub, 2)

    def dot(lo, hi, rhs):
        return jnp.dot(onehot[lo:hi, :], rhs, preferred_element_type=jnp.float32)

    own = dot(0, 256, own_in)
    pairs = dot(256, 384, pair_in)
    sides = dot(384, 528, side_in)

    def tile(x, at):
        return x[at * 8 : at * 8 + 8, :]

    def put_side(cells, rows):
        for a, e in rows:
            right = pltpu.roll(cells, (128 - 16 * a) % 128, 1)
            left = pltpu.roll(cells, (112 - 16 * a) % 128, 1)
            u0[e, :, 128:256] = jnp.where(lane < 4, right, jnp.where(lane >= 124, left, 0.0))

    for tx in range(4):
        rows = swap_blocks([tile(own, tx * 8 + ty) for ty in range(8)])
        for a in range(8):
            u0[4 + tx * 8 + a, :, 0:128] = rows[a]
        r = tile(sides, tx) + pltpu.roll(tile(sides, 4 + tx), 124, 1)
        l = tile(sides, 8 + tx) + pltpu.roll(tile(sides, 12 + tx), 4, 1)
        put_side(jnp.where(b_of < 4, r, l), [(a, 4 + tx * 8 + a) for a in range(8)])
    rows = swap_blocks([tile(pairs, ty) for ty in range(8)])
    for a in range(4):
        u0[36 + a, :, 0:128] = rows[a]
    rows = swap_blocks([tile(pairs, 8 + ty) for ty in range(8)])
    for a in range(4, 8):
        u0[a - 4, :, 0:128] = rows[a]
    put_side(tile(sides, 16), [(a, 36 + a) for a in range(4)] + [(a, a - 4) for a in range(4, 8)])

    above, below, before, after = sides_of(from_c, from_x, from_a, from_b)

    def flag(du, dv):
        return jnp.where(neighbour(du, dv) < OWNERS, 1.0, 0.0)

    def corner(du, dv):
        s = neighbour(du, dv)
        z = recv[jnp.minimum(s, OWNERS - 1), 2].astype(jnp.float32)[8:16, :]
        z = jnp.where(s < OWNERS, z, 0.0)
        left = pltpu.roll(z, 4, 1) + pltpu.roll(z, 8, 1)
        right = pltpu.roll(z, 124, 1) + pltpu.roll(z, 120, 1)
        return left if dv < 0 else right

    def ends(left, right):
        return jnp.where(lane < 4, right, jnp.where(lane >= 124, left, 0.0))

    dext[0:8, 0:128] = above(40, 48) * flag(-1, 0)
    dext[40:48, 0:128] = below(16, 24) * flag(1, 0)
    dext[8:40, 0:128] = diff[...]
    dext[0:8, 128:256] = ends(corner(-1, -1), corner(-1, 1))
    dext[40:48, 128:256] = ends(corner(1, -1), corner(1, 1))
    for q in range(4):
        dext[8 + q * 8 : 16 + q * 8, 128:256] = ends(
            before(8 + q * 8, 16 + q * 8) * flag(0, -1), after(8 + q * 8, 16 + q * 8) * flag(0, 1)
        )

    src, dst = u0, u1
    for sweep in range(SWEEPS):
        for e in range(sweep + 1, 39 - sweep):
            u = src[e]
            beside = src[e + 1] + src[e - 1] + pltpu.roll(u, 255, 1) + pltpu.roll(u, 1, 1)
            d = jnp.broadcast_to(dext[e + 4 : e + 5, :], (8, 256))
            new = u + d * (beside - 4.0 * u)
            if sweep < SWEEPS - 1:
                dst[e] = new
            else:
                out[pl.ds(e - 4, 8, stride=OXD), :] = new[:, :128]
        src, dst = dst, src


def local(flux, diffusivity, remap_bank, rec_owner, rec_source, rec_target, rec_weight):
    vmem = pl.BlockSpec(memory_space=pltpu.VMEM)
    smem = pl.BlockSpec(memory_space=pltpu.SMEM)
    anywhere = pl.BlockSpec(memory_space=pl.ANY)
    flux_rows = flux.reshape(F * AXD, AYD)
    flux_scratch = [pltpu.VMEM((2, F * AXD, 128), jnp.float32), pltpu.SemaphoreType.DMA((2,))]
    records = [x.reshape(1, RECS) for x in (rec_owner, rec_source, rec_target, rec_weight)]
    f32, i32 = jnp.float32, jnp.int32
    to_c, to_x, to_a, to_b, tab = pl.pallas_call(
        prepare_kernel,
        out_shape=[jax.ShapeDtypeStruct((48, 128), f32)] * 2
        + [jax.ShapeDtypeStruct((40, 128), f32)] * 2
        + [jax.ShapeDtypeStruct((TAB_ROWS, RECS), i32)],
        in_specs=[anywhere] + [vmem] * 5,
        out_specs=[vmem] * 5,
        scratch_shapes=flux_scratch,
        name="prepare",
    )(flux_rows, diffusivity, *records)

    def swap(x, axis, count, odd):
        return lax.ppermute(x, axis, [(i, (((i + odd) ^ 1) - odd) % count) for i in range(count)])

    came = []
    for x, axis, count, odd in ((to_c, "gx", NGX, 0), (to_x, "gx", NGX, 1), (to_a, "gy", NGY, 0), (to_b, "gy", NGY, 1)):
        came.append(swap(x, axis, count, odd))

    outgoing = pl.pallas_call(
        send_kernel,
        out_shape=jax.ShapeDtypeStruct((OWNERS, 3, 16, 128), jnp.bfloat16),
        in_specs=[smem, vmem, anywhere] + [vmem] * 6,
        out_specs=vmem,
        scratch_shapes=[
            pltpu.VMEM((512, 768), jnp.bfloat16),
            pltpu.VMEM((NWB * 512, 128), f32),
            pltpu.VMEM((OWNERS * 16, 128), f32),
            pltpu.VMEM((OWNERS * 16 + 16, 128), f32),
            pltpu.VMEM((OWNERS * 8 + 8, 128), f32),
            pltpu.VMEM((OWNERS * 16 + 16, 128), f32),
            pltpu.VMEM((OWNERS, 128), f32),
        ]
        + flux_scratch,
        name="remap_send",
    )(tab, tab, flux_rows, *came, diffusivity, remap_bank.reshape(NWB, 768, 128))
    arrived = lax.all_to_all(outgoing, ("gx", "gy"), split_axis=0, concat_axis=0, tiled=True)
    ocean = pl.pallas_call(
        ocean_kernel,
        out_shape=jax.ShapeDtypeStruct((F * OXD, OYD), f32),
        in_specs=[vmem] * 6,
        out_specs=vmem,
        scratch_shapes=[
            pltpu.VMEM((528, OWNERS * 16), jnp.bfloat16),
            pltpu.VMEM((48, 256), f32),
            pltpu.VMEM((40, 8, 256), f32),
            pltpu.VMEM((40, 8, 256), f32),
        ],
        name="ocean",
    )(arrived, diffusivity, *came)
    return ocean.reshape(F, OXD, OYD)


def solution(mesh):
    in_specs = (
        P(None, "gx", "gy"),
        P("gx", "gy"),
        P(),
        P(("gx", "gy")),
        P(("gx", "gy")),
        P(("gx", "gy")),
        P(("gx", "gy")),
    )
    return jax.shard_map(local, mesh=mesh, in_specs=in_specs, out_specs=P(None, "gx", "gy"), check_vma=False)
```

```python
import jax
import jax.numpy as jnp
from jax import lax
from jax.experimental import pallas as pl
from jax.experimental.pallas import tpu as pltpu
from jax.sharding import PartitionSpec as P


F = 8
AXD, AYD = 64, 256
OXD, OYD = 32, 128
NWB = 16
RECS = 128
SWEEPS = 4
OWNERS = 128
NGX, NGY = 8, 16
(PROD, OWN, XROW, YROW, CROW, KX, YQ, CC, SHIFT, OWNER, XTO, YTO, PO, PX, PY, VO, VX, VY) = range(18)
TAB_ROWS = 24
ABSENT = 256.0
CORNERS = ((-1, -1), (-1, 1), (1, -1), (1, 1))


def lanes(shape):
    return lax.broadcasted_iota(jnp.int32, shape, 1)


def swap_blocks(v):
    block = lanes(v[0].shape) // 16
    for s in range(3):
        d = 1 << s
        high = (block & d) != 0
        n = list(v)
        for p in range(8):
            if not p & d:
                a, b = v[p], v[p | d]
                if d == 4:
                    up = down = pltpu.roll(jnp.where(high, a, b), 64, 1)
                else:
                    up, down = pltpu.roll(b, 16 * d, 1), pltpu.roll(a, 128 - 16 * d, 1)
                n[p] = jnp.where(high, up, a)
                n[p | d] = jnp.where(high, b, down)
        v = n
    return v


def neighbour(du, dv):
    gx, gy = lax.axis_index("gx") + du, lax.axis_index("gy") + dv
    return jnp.where((gx >= 0) & (gx < NGX) & (gy >= 0) & (gy < NGY), gx * NGY + gy, OWNERS)


def even(axis):
    return lax.axis_index(axis) % 2 == 0


def sides_of(from_c, from_x, from_a, from_b):
    even_x, even_y = even("gx"), even("gy")
    return (
        lambda lo, hi: jnp.where(even_x, from_x[lo:hi, :], from_c[lo:hi, :]),
        lambda lo, hi: jnp.where(even_x, from_c[lo:hi, :], from_x[lo:hi, :]),
        lambda lo, hi: jnp.where(even_y, from_b[lo:hi, :], from_a[lo:hi, :]),
        lambda lo, hi: jnp.where(even_y, from_a[lo:hi, :], from_b[lo:hi, :]),
    )


def prepare_kernel(flux_in, diff_in, ids, to_c, to_x, to_a, to_b, tab, flux, diff, sems):
    moves = [(diff_in, diff)] + [(flux_in.at[:, pl.ds(g * 128, 128)], flux.at[g]) for g in range(2)]
    copies = [pltpu.make_async_copy(src, dst, sems.at[n]) for n, (src, dst) in enumerate(moves)]
    for copy in copies:
        copy.start()
    lane = lanes((8, 128))
    owner, source, target, weight = (ids[n : n + 1, :] for n in range(4))
    across = jnp.broadcast_to(owner, (RECS, RECS))
    along = jnp.transpose(across.astype(jnp.float32)).astype(jnp.int32)
    sub = lax.broadcasted_iota(jnp.int32, (RECS, RECS), 0)
    earlier = jnp.where((across == along) & (sub < lanes((RECS, RECS))), 1.0, 0.0)
    slot = jnp.sum(earlier, axis=0, keepdims=True).astype(jnp.int32)
    ox, oy = owner >> 4, owner & 15
    tx, ty = target >> 3, target & 7
    sx = jnp.where(tx == 0, -1, jnp.where(tx == 3, 1, 0))
    sy = jnp.where(ty == 0, -1, jnp.where(ty == 7, 1, 0))
    ok_x = (sx != 0) & (ox + sx >= 0) & (ox + sx < NGX)
    ok_y = (sy != 0) & (oy + sy >= 0) & (oy + sy < NGY)
    dx = jnp.where(ok_x, owner + sx * NGY, OWNERS)
    dy = jnp.where(ok_y, owner + sy, OWNERS)
    dc = jnp.where(ok_x & ok_y, owner + sx * NGY + sy, OWNERS)
    kx = jnp.where(tx == 3, 1, 0)
    ky = jnp.where(ty == 7, 1, 0)
    ti, tj = source >> 4, source & 15
    t8 = (ti * 16 + (tj & 7) * 2 + (tj >> 3)) * 8
    rows = [
        weight * 512 + t8, owner * 16 + slot * 8, dx * 16 + slot * 8, dy * 8, dc * 16 + slot * 8,
        kx, jnp.where(ky == 0, slot, 3 - slot), kx * 4 + ky * 3, jnp.where(ky == 0, 4 * slot, (128 - 4 * slot) & 127),
        owner, dx, dy, 36 + slot, 38 + 2 * kx + slot, jnp.where(ky == 0, 42, 52) + slot,
        target * 8 + 1, ty * 8 + 1, tx * 8 + 1,
    ]
    for n, value in enumerate(rows):
        tab[n : n + 1, :] = value
    for n in range(len(rows), TAB_ROWS):
        tab[n : n + 1, :] = slot

    copies[0].wait()
    for to in (to_c, to_x):
        to[16:48, :] = diff[...]
    for to in (to_a, to_b):
        to[8:40, :] = diff[...]
    for copy in copies[1:]:
        copy.wait()

    def row(i, g):
        return flux[g, pl.ds(i, 8, stride=AXD), :]

    even_x, even_y = even("gx"), even("gy")
    for g in range(2):
        bottom, top = row(AXD - 1, g), row(0, g)
        to_c[g * 8 : g * 8 + 8, :] = jnp.where(even_x, bottom, top)
        to_x[g * 8 : g * 8 + 8, :] = jnp.where(even_x, top, bottom)
    last = jnp.zeros((8, 128), jnp.float32)
    first = jnp.zeros((8, 128), jnp.float32)
    for i in range(AXD):
        last = jnp.where(lane == i, row(i, 1)[:, 127:128], last)
        first = jnp.where(lane == i, row(i, 0)[:, 0:1], first)
    to_a[0:8, :] = jnp.where(even_y, last, first)
    to_b[0:8, :] = jnp.where(even_y, first, last)


def tiles_kernel(flux, tabv, bank_in, lhs, lab, bank, sem):
    weights = pltpu.make_async_copy(bank_in, bank, sem)
    weights.start()
    rows3 = lax.broadcasted_iota(jnp.int32, (128, 3 * RECS), 0)

    def three(*at):
        return jnp.concatenate([jnp.broadcast_to(tabv[n : n + 1, :], (128, RECS)) for n in at], axis=1)

    going = jnp.where(three(OWNER, XTO, YTO) == rows3, 1.0, 0.0).astype(jnp.bfloat16)
    label = jnp.where(three(PO, PX, PY) == rows3, three(VO, VX, VY), 0).astype(jnp.float32).astype(jnp.bfloat16)
    lab[...] = lax.dot_general(going, label, (((1,), (1,)), ((), ())), preferred_element_type=jnp.float32)

    wide = lanes((8, 256))
    outside = jnp.zeros((8, 256), jnp.float32)

    def row(i):
        if i < 0 or i >= AXD:
            return outside
        return jnp.concatenate([flux[g, pl.ds(i, 8, stride=AXD), :] for g in range(2)], axis=1)

    for ti in range(4):
        x = [row(i) for i in range(ti * 16 - 1, ti * 16 + 17)]
        for k in range(3):
            vals = []
            for a in range(16):
                if k == 0:
                    vals.append(x[a + 1])
                elif k == 1:
                    vals.append((x[a + 2] - x[a]) * 0.5)
                else:
                    nxt = jnp.where(wide == 255, 0.0, pltpu.roll(x[a + 1], 255, 1))
                    prv = jnp.where(wide == 0, 0.0, pltpu.roll(x[a + 1], 1, 1))
                    vals.append((nxt - prv) * 0.5)
            for h in range(2):
                packed = [
                    jnp.concatenate([vals[h * 8 + q][:, :128], vals[h * 8 + q][:, 128:]], axis=0).astype(jnp.bfloat16)
                    for q in range(8)
                ]
                for q, tile in enumerate(swap_blocks(packed)):
                    lhs[pl.ds((ti * 8 + q) * 16, 16), pl.ds(k * 256 + h * 128, 128)] = tile
    weights.wait()


def send_kernel(
    tab_in, lhs_in, lab, from_c, from_x, from_a, from_b, diff, bank, out,
    tab, lhs, prod, owns, pairs, sides, corners, sems,
):
    copies = [pltpu.make_async_copy(src, dst, sems.at[n]) for n, (src, dst) in enumerate(((tab_in, tab), (lhs_in, lhs)))]
    for copy in copies:
        copy.start()
    lane = lanes((8, 128))
    sub = lax.broadcasted_iota(jnp.int32, (8, 128), 0)
    a_of, b_of = lane // 16, lane % 16
    is_label = (a_of == 2) & (b_of >= 4) & (b_of < 12) | (a_of == 3) & (b_of >= 4) & (b_of < 6)
    absent = jnp.where(is_label, ABSENT, 0.0)
    offset = (sub - 1).astype(jnp.float32)

    zero = jnp.zeros((8, 128), jnp.float32)

    def clear(o, carry):
        at = pl.multiple_of(o * 16, 16)
        half = pl.multiple_of(o * 8, 8)
        owns[pl.ds(at, 8), :] = zero
        owns[pl.ds(at + 8, 8), :] = zero
        pairs[pl.ds(at, 8), :] = zero
        pairs[pl.ds(at + 8, 8), :] = zero
        sides[pl.ds(half, 8), :] = zero
        corners[pl.ds(at, 8), :] = zero
        corners[pl.ds(at + 8, 8), :] = zero
        return carry

    lax.fori_loop(0, OWNERS, clear, 0, unroll=4)
    for copy in copies:
        copy.wait()

    above, below, before, after = sides_of(from_c, from_x, from_a, from_b)
    lane16 = lanes((16, 128))

    def add(ti, q, k, h, lo, hi, what):
        rows_at, cols_at = pl.ds((ti * 8 + q) * 16, 16), pl.ds(k * 256 + h * 128, 128)
        if hi - lo == 8:
            none = jnp.zeros((8, 128), jnp.float32)
            what = jnp.concatenate([what, none] if lo == 0 else [none, what], axis=0)
        lhs[rows_at, cols_at] = (lhs[rows_at, cols_at].astype(jnp.float32) + what).astype(jnp.bfloat16)

    top, bottom = above(0, 16) * -0.5, below(0, 16) * 0.5
    for q in range(8):
        add(0, q, 1, 0, 0, 16, jnp.where(lane16 < 16, pltpu.roll(top, (128 - 16 * q) % 128, 1), 0.0))
        add(3, q, 1, 1, 0, 16, jnp.where(lane16 >= 112, pltpu.roll(bottom, 112 - 16 * q, 1), 0.0))
    left, right = before(0, 8) * -0.5, after(0, 8) * 0.5
    for ti in range(4):
        for h in range(2):
            low = jnp.zeros((8, 128), jnp.float32)
            high = jnp.zeros((8, 128), jnp.float32)
            for q in range(8):
                i = ti * 16 + h * 8 + q
                low = jnp.where(lane == q * 16, left[:, i : i + 1], low)
                high = jnp.where(lane == q * 16 + 15, right[:, i : i + 1], high)
            add(ti, 0, 2, h, 0, 8, low)
            add(ti, 7, 2, h, 8, 16, high)

    def product(n, carry):
        rhs = jnp.concatenate([bank[2 * n], bank[2 * n + 1]], axis=1)
        res = jnp.dot(lhs[...], rhs, preferred_element_type=jnp.float32)
        at = pl.multiple_of(n * 1024, 1024)
        prod[pl.ds(at, 512), :] = res[:, :128]
        prod[pl.ds(at + 512, 512), :] = res[:, 128:]
        return carry

    lax.fori_loop(0, NWB // 2, product, 0)

    half_of, quarter_of = lane // 64, b_of // 4
    code = half_of * 4 + quarter_of

    def rows(ref, at):
        return ref.at[pl.ds(pl.multiple_of(at, 8), 8), :]

    for r in range(RECS):
        value = rows(prod, tab[PROD, r])[...]
        rows(owns, tab[OWN, r])[...] = value
        pltpu.store(rows(pairs, tab[XROW, r]), value, mask=half_of == tab[KX, r])
        pltpu.store(rows(sides, tab[YROW, r]), pltpu.roll(value, tab[SHIFT, r], 1), mask=quarter_of == tab[YQ, r])
        pltpu.store(rows(corners, tab[CROW, r]), value, mask=code == tab[CC, r])

    for du, dv in CORNERS:
        first = 0 if du < 0 else 24
        cells = diff[first : first + 8, :]
        high = cells.astype(jnp.bfloat16).astype(jnp.float32)
        low = cells - high
        to = rows(corners, neighbour(du, dv) * 16)
        if dv < 0:
            pltpu.store(to, pltpu.roll(high, 4, 1), mask=(lane >= 4) & (lane < 8))
            pltpu.store(to, pltpu.roll(low, 8, 1), mask=(lane >= 8) & (lane < 12))
        else:
            pltpu.store(to, pltpu.roll(high, 124, 1), mask=(lane >= 120) & (lane < 124))
            pltpu.store(to, pltpu.roll(low, 120, 1), mask=(lane >= 116) & (lane < 120))

    def convert(o, carry):
        at = pl.multiple_of(o * 16, 16)
        half = pl.ds(pl.multiple_of(o * 8, 8), 8)
        found = jnp.broadcast_to(lab[pl.ds(o, 1), :], (8, 128))
        tags = jnp.where(found > 0, found + offset, absent)
        last = tags + (corners[pl.ds(at, 8), :] + corners[pl.ds(at + 8, 8), :])
        out[o, 0] = owns[pl.ds(at, 16), :].astype(jnp.bfloat16)
        out[o, 1] = pairs[pl.ds(at, 16), :].astype(jnp.bfloat16)
        out[o, 2] = jnp.concatenate([sides[half, :], last], axis=0).astype(jnp.bfloat16)
        return carry

    lax.fori_loop(0, OWNERS, convert, 0, unroll=8)


def ocean_kernel(recv, diff, from_c, from_x, from_a, from_b, out, onehot, dext, u0, u1):
    lane = lanes((8, 128))
    b_of = lane % 16
    K = OWNERS * 16
    own_in = recv[:, 0].reshape(K, 128)
    pair_in = recv[:, 1].reshape(K, 128)
    side_in = recv[:, 2].reshape(K, 128)

    pick_row = lax.broadcasted_iota(jnp.int32, (16, 128), 0)
    pick_lane = lanes((16, 128))
    label_lane = jnp.where(pick_row < 8, 36 + pick_row, 44 + pick_row)
    pick = ((label_lane == pick_lane) & (pick_row < 10)).astype(jnp.float32).astype(jnp.bfloat16)
    keys = lax.dot_general(pick, side_in, (((1,), (1,)), ((), ())), preferred_element_type=jnp.float32)
    early = pltpu.roll(keys, K - 8, 1)
    klane = lanes((8, K))
    sub = lax.broadcasted_iota(jnp.int32, (8, K), 0).astype(jnp.float32)
    late = (klane & 8) != 0

    def spread(rows, at):
        return jnp.broadcast_to(rows[at : at + 1, :], (8, K))

    def both(at):
        return jnp.where(late, spread(keys, at + 1), spread(early, at)) - sub

    def first(at):
        return jnp.where(late, -1000.0, spread(early, at)) - sub

    def hot(base, key, count):
        for t in range(0, count, 2):
            pair = [jnp.where(key == 8.0 * (t + q), 1.0, 0.0) for q in range(2)]
            onehot[pl.ds(base + t * 8, 16), :] = jnp.concatenate(pair, axis=0).astype(jnp.bfloat16)

    hot(0, both(0), 32)
    hot(256, both(2), 8)
    hot(320, both(4), 8)
    hot(384, first(6), 4)
    hot(416, first(7), 4)
    hot(448, first(8), 4)
    hot(480, first(9), 4)
    hot(512, jnp.where(late, (klane & 7).astype(jnp.float32), -1000.0) - sub, 2)

    def dot(lo, hi, rhs):
        return jnp.dot(onehot[lo:hi, :], rhs, preferred_element_type=jnp.float32)

    own = dot(0, 256, own_in)
    pairs = dot(256, 384, pair_in)
    sides = dot(384, 528, side_in)

    def tile(x, at):
        return x[at * 8 : at * 8 + 8, :]

    def put_side(cells, rows):
        for a, e in rows:
            right = pltpu.roll(cells, (128 - 16 * a) % 128, 1)
            left = pltpu.roll(cells, (112 - 16 * a) % 128, 1)
            u0[e, :, 128:256] = jnp.where(lane < 4, right, jnp.where(lane >= 124, left, 0.0))

    for tx in range(4):
        rows = swap_blocks([tile(own, tx * 8 + ty) for ty in range(8)])
        for a in range(8):
            u0[4 + tx * 8 + a, :, 0:128] = rows[a]
        r = tile(sides, tx) + pltpu.roll(tile(sides, 4 + tx), 124, 1)
        l = tile(sides, 8 + tx) + pltpu.roll(tile(sides, 12 + tx), 4, 1)
        put_side(jnp.where(b_of < 4, r, l), [(a, 4 + tx * 8 + a) for a in range(8)])
    rows = swap_blocks([tile(pairs, ty) for ty in range(8)])
    for a in range(4):
        u0[36 + a, :, 0:128] = rows[a]
    rows = swap_blocks([tile(pairs, 8 + ty) for ty in range(8)])
    for a in range(4, 8):
        u0[a - 4, :, 0:128] = rows[a]
    put_side(tile(sides, 16), [(a, 36 + a) for a in range(4)] + [(a, a - 4) for a in range(4, 8)])

    above, below, before, after = sides_of(from_c, from_x, from_a, from_b)

    def flag(du, dv):
        return jnp.where(neighbour(du, dv) < OWNERS, 1.0, 0.0)

    def corner(du, dv):
        s = neighbour(du, dv)
        z = recv[jnp.minimum(s, OWNERS - 1), 2].astype(jnp.float32)[8:16, :]
        z = jnp.where(s < OWNERS, z, 0.0)
        left = pltpu.roll(z, 4, 1) + pltpu.roll(z, 8, 1)
        right = pltpu.roll(z, 124, 1) + pltpu.roll(z, 120, 1)
        return left if dv < 0 else right

    def ends(left, right):
        return jnp.where(lane < 4, right, jnp.where(lane >= 124, left, 0.0))

    dext[0:8, 0:128] = above(40, 48) * flag(-1, 0)
    dext[40:48, 0:128] = below(16, 24) * flag(1, 0)
    dext[8:40, 0:128] = diff[...]
    dext[0:8, 128:256] = ends(corner(-1, -1), corner(-1, 1))
    dext[40:48, 128:256] = ends(corner(1, -1), corner(1, 1))
    for q in range(4):
        dext[8 + q * 8 : 16 + q * 8, 128:256] = ends(
            before(8 + q * 8, 16 + q * 8) * flag(0, -1), after(8 + q * 8, 16 + q * 8) * flag(0, 1)
        )

    src, dst = u0, u1
    for sweep in range(SWEEPS):
        for e in range(sweep + 1, 39 - sweep):
            u = src[e]
            beside = src[e + 1] + src[e - 1] + pltpu.roll(u, 255, 1) + pltpu.roll(u, 1, 1)
            d = jnp.broadcast_to(dext[e + 4 : e + 5, :], (8, 256))
            new = u + d * (beside - 4.0 * u)
            if sweep < SWEEPS - 1:
                dst[e] = new
            else:
                out[pl.ds(e - 4, 8, stride=OXD), :] = new[:, :128]
        src, dst = dst, src


def local(flux, diffusivity, remap_bank, rec_owner, rec_source, rec_target, rec_weight):
    vmem = pl.BlockSpec(memory_space=pltpu.VMEM)
    smem = pl.BlockSpec(memory_space=pltpu.SMEM)
    anywhere = pl.BlockSpec(memory_space=pl.ANY)
    flux_rows = flux.reshape(F * AXD, AYD)
    hbm = pl.BlockSpec(memory_space=pltpu.HBM)
    records = jnp.stack([rec_owner, rec_source, rec_target, rec_weight])
    f32, i32 = jnp.float32, jnp.int32
    to_c, to_x, to_a, to_b, tab, flux_halves, diff = pl.pallas_call(
        prepare_kernel,
        out_shape=[jax.ShapeDtypeStruct((48, 128), f32)] * 2
        + [jax.ShapeDtypeStruct((40, 128), f32)] * 2
        + [jax.ShapeDtypeStruct((TAB_ROWS, RECS), i32), jax.ShapeDtypeStruct((2, F * AXD, 128), f32)]
        + [jax.ShapeDtypeStruct((OXD, OYD), f32)],
        in_specs=[hbm] * 2 + [vmem],
        out_specs=[vmem] * 7,
        scratch_shapes=[pltpu.SemaphoreType.DMA((3,))],
        name="prepare",
        compiler_params=pltpu.CompilerParams(vmem_limit_bytes=6 << 20),
    )(flux_rows, diffusivity, records)

    def swap(x, axis, count, odd):
        return lax.ppermute(x, axis, [(i, (((i + odd) ^ 1) - odd) % count) for i in range(count)])

    came = []
    for x, axis, count, odd in ((to_c, "gx", NGX, 0), (to_x, "gx", NGX, 1), (to_a, "gy", NGY, 0), (to_b, "gy", NGY, 1)):
        came.append(swap(x, axis, count, odd))

    bf16 = jnp.bfloat16
    lhs, lab, bank = pl.pallas_call(
        tiles_kernel,
        out_shape=[jax.ShapeDtypeStruct((512, 768), bf16), jax.ShapeDtypeStruct((OWNERS, 128), f32)]
        + [jax.ShapeDtypeStruct((NWB, 768, 128), bf16)],
        in_specs=[vmem, vmem, hbm],
        out_specs=[vmem] * 3,
        scratch_shapes=[pltpu.SemaphoreType.DMA],
        name="tiles",
    compiler_params=pltpu.CompilerParams(vmem_limit_bytes=8 << 20),
    )(flux_halves, tab, remap_bank.reshape(NWB, 768, 128))

    outgoing = pl.pallas_call(
        send_kernel,
        out_shape=jax.ShapeDtypeStruct((OWNERS, 3, 16, 128), bf16),
        in_specs=[anywhere] * 2 + [vmem] * 7,
        out_specs=vmem,
        scratch_shapes=[
            pltpu.SMEM((TAB_ROWS, RECS), i32),
            pltpu.VMEM((512, 768), bf16),
            pltpu.VMEM((NWB * 512, 128), f32),
            pltpu.VMEM((OWNERS * 16, 128), f32),
            pltpu.VMEM((OWNERS * 16 + 16, 128), f32),
            pltpu.VMEM((OWNERS * 8 + 8, 128), f32),
            pltpu.VMEM((OWNERS * 16 + 16, 128), f32),
            pltpu.SemaphoreType.DMA((2,)),
        ],
        name="remap_send",
        compiler_params=pltpu.CompilerParams(vmem_limit_bytes=24 << 20),
    )(tab, lhs, lab, *came, diff, bank)
    arrived = lax.all_to_all(outgoing, ("gx", "gy"), split_axis=0, concat_axis=0, tiled=True)
    ocean = pl.pallas_call(
        ocean_kernel,
        out_shape=jax.ShapeDtypeStruct((F * OXD, OYD), f32),
        in_specs=[vmem] * 6,
        out_specs=vmem,
        scratch_shapes=[
            pltpu.VMEM((528, OWNERS * 16), jnp.bfloat16),
            pltpu.VMEM((48, 256), f32),
            pltpu.VMEM((40, 8, 256), f32),
            pltpu.VMEM((40, 8, 256), f32),
        ],
        name="ocean",
        compiler_params=pltpu.CompilerParams(vmem_limit_bytes=16 << 20),
    )(arrived, diff, *came)
    return ocean.reshape(F, OXD, OYD)


def solution(mesh):
    in_specs = (
        P(None, "gx", "gy"),
        P("gx", "gy"),
        P(),
        P(("gx", "gy")),
        P(("gx", "gy")),
        P(("gx", "gy")),
        P(("gx", "gy")),
    )
    return jax.shard_map(local, mesh=mesh, in_specs=in_specs, out_specs=P(None, "gx", "gy"), check_vma=False)
```

```python
import jax
import jax.numpy as jnp
from jax import lax
from jax.experimental import pallas as pl
from jax.experimental.pallas import tpu as pltpu
from jax.sharding import PartitionSpec as P


F = 8
AXD, AYD = 64, 256
OXD, OYD = 32, 128
NWB = 16
RECS = 128
SWEEPS = 4
OWNERS = 128
NGX, NGY = 8, 16
(PROD, OWN, XROW, YROW, CROW, KX, YQ, CC, SHIFT, OWNER, XTO, YTO, PO, PX, PY, VO, VX, VY) = range(18)
TAB_ROWS = 24
ABSENT = 256.0
CORNERS = ((-1, -1), (-1, 1), (1, -1), (1, 1))


def lanes(shape):
    return lax.broadcasted_iota(jnp.int32, shape, 1)


def swap_blocks(v):
    block = lanes(v[0].shape) // 16
    for s in range(3):
        d = 1 << s
        high = (block & d) != 0
        n = list(v)
        for p in range(8):
            if not p & d:
                a, b = v[p], v[p | d]
                if d == 4:
                    up = down = pltpu.roll(jnp.where(high, a, b), 64, 1)
                else:
                    up, down = pltpu.roll(b, 16 * d, 1), pltpu.roll(a, 128 - 16 * d, 1)
                n[p] = jnp.where(high, up, a)
                n[p | d] = jnp.where(high, b, down)
        v = n
    return v


def neighbour(du, dv):
    gx, gy = lax.axis_index("gx") + du, lax.axis_index("gy") + dv
    return jnp.where((gx >= 0) & (gx < NGX) & (gy >= 0) & (gy < NGY), gx * NGY + gy, OWNERS)


def even(axis):
    return lax.axis_index(axis) % 2 == 0


def sides_of(from_c, from_x, from_a, from_b):
    even_x, even_y = even("gx"), even("gy")
    return (
        lambda lo, hi: jnp.where(even_x, from_x[lo:hi, :], from_c[lo:hi, :]),
        lambda lo, hi: jnp.where(even_x, from_c[lo:hi, :], from_x[lo:hi, :]),
        lambda lo, hi: jnp.where(even_y, from_b[lo:hi, :], from_a[lo:hi, :]),
        lambda lo, hi: jnp.where(even_y, from_a[lo:hi, :], from_b[lo:hi, :]),
    )


def prepare_kernel(flux_in, diff_in, owner_in, source_in, target_in, weight_in, to_c, to_x, to_a, to_b, tab, flux, diff, ids, sems):
    moves = [(x, ids.at[n]) for n, x in enumerate((owner_in, source_in, target_in, weight_in))]
    moves += [(diff_in, diff)] + [(flux_in.at[:, pl.ds(g * 128, 128)], flux.at[g]) for g in range(2)]
    copies = [pltpu.make_async_copy(src, dst, sems.at[n]) for n, (src, dst) in enumerate(moves)]
    for copy in copies:
        copy.start()
    lane = lanes((8, 128))
    for copy in copies[:5]:
        copy.wait()
    owner, source, target, weight = (ids[n] for n in range(4))
    across = jnp.broadcast_to(owner, (RECS, RECS))
    along = jnp.transpose(across.astype(jnp.float32)).astype(jnp.int32)
    sub = lax.broadcasted_iota(jnp.int32, (RECS, RECS), 0)
    earlier = jnp.where((across == along) & (sub < lanes((RECS, RECS))), 1.0, 0.0)
    slot = jnp.sum(earlier, axis=0, keepdims=True).astype(jnp.int32)
    ox, oy = owner >> 4, owner & 15
    tx, ty = target >> 3, target & 7
    sx = jnp.where(tx == 0, -1, jnp.where(tx == 3, 1, 0))
    sy = jnp.where(ty == 0, -1, jnp.where(ty == 7, 1, 0))
    ok_x = (sx != 0) & (ox + sx >= 0) & (ox + sx < NGX)
    ok_y = (sy != 0) & (oy + sy >= 0) & (oy + sy < NGY)
    dx = jnp.where(ok_x, owner + sx * NGY, OWNERS)
    dy = jnp.where(ok_y, owner + sy, OWNERS)
    dc = jnp.where(ok_x & ok_y, owner + sx * NGY + sy, OWNERS)
    kx = jnp.where(tx == 3, 1, 0)
    ky = jnp.where(ty == 7, 1, 0)
    ti, tj = source >> 4, source & 15
    t8 = (ti * 16 + (tj & 7) * 2 + (tj >> 3)) * 8
    rows = [
        weight * 512 + t8, owner * 16 + slot * 8, dx * 16 + slot * 8, dy * 8, dc * 16 + slot * 8,
        kx, jnp.where(ky == 0, slot, 3 - slot), kx * 4 + ky * 3, jnp.where(ky == 0, 4 * slot, (128 - 4 * slot) & 127),
        owner, dx, dy, 36 + slot, 38 + 2 * kx + slot, jnp.where(ky == 0, 42, 52) + slot,
        target * 8 + 1, ty * 8 + 1, tx * 8 + 1,
    ]
    for n, value in enumerate(rows):
        tab[n : n + 1, :] = value
    for n in range(len(rows), TAB_ROWS):
        tab[n : n + 1, :] = slot

    for to in (to_c, to_x):
        to[16:48, :] = diff[...]
    for to in (to_a, to_b):
        to[8:40, :] = diff[...]
    for copy in copies[5:]:
        copy.wait()

    def row(i, g):
        return flux[g, pl.ds(i, 8, stride=AXD), :]

    even_x, even_y = even("gx"), even("gy")
    for g in range(2):
        bottom, top = row(AXD - 1, g), row(0, g)
        to_c[g * 8 : g * 8 + 8, :] = jnp.where(even_x, bottom, top)
        to_x[g * 8 : g * 8 + 8, :] = jnp.where(even_x, top, bottom)
    last = jnp.zeros((8, 128), jnp.float32)
    first = jnp.zeros((8, 128), jnp.float32)
    for i in range(AXD):
        last = jnp.where(lane == i, row(i, 1)[:, 127:128], last)
        first = jnp.where(lane == i, row(i, 0)[:, 0:1], first)
    to_a[0:8, :] = jnp.where(even_y, last, first)
    to_b[0:8, :] = jnp.where(even_y, first, last)


def tiles_kernel(flux, tabv, bank_in, lhs, lab, bank, sem):
    weights = pltpu.make_async_copy(bank_in, bank, sem)
    weights.start()
    rows3 = lax.broadcasted_iota(jnp.int32, (128, 3 * RECS), 0)

    def three(*at):
        return jnp.concatenate([jnp.broadcast_to(tabv[n : n + 1, :], (128, RECS)) for n in at], axis=1)

    going = jnp.where(three(OWNER, XTO, YTO) == rows3, 1.0, 0.0).astype(jnp.bfloat16)
    label = jnp.where(three(PO, PX, PY) == rows3, three(VO, VX, VY), 0).astype(jnp.float32).astype(jnp.bfloat16)
    lab[...] = lax.dot_general(going, label, (((1,), (1,)), ((), ())), preferred_element_type=jnp.float32)

    wide = lanes((8, 256))
    outside = jnp.zeros((8, 256), jnp.float32)

    def row(i):
        if i < 0 or i >= AXD:
            return outside
        return jnp.concatenate([flux[g, pl.ds(i, 8, stride=AXD), :] for g in range(2)], axis=1)

    for ti in range(4):
        x = [row(i) for i in range(ti * 16 - 1, ti * 16 + 17)]
        for k in range(3):
            vals = []
            for a in range(16):
                if k == 0:
                    vals.append(x[a + 1])
                elif k == 1:
                    vals.append((x[a + 2] - x[a]) * 0.5)
                else:
                    nxt = jnp.where(wide == 255, 0.0, pltpu.roll(x[a + 1], 255, 1))
                    prv = jnp.where(wide == 0, 0.0, pltpu.roll(x[a + 1], 1, 1))
                    vals.append((nxt - prv) * 0.5)
            for h in range(2):
                packed = [
                    jnp.concatenate([vals[h * 8 + q][:, :128], vals[h * 8 + q][:, 128:]], axis=0).astype(jnp.bfloat16)
                    for q in range(8)
                ]
                for q, tile in enumerate(swap_blocks(packed)):
                    lhs[pl.ds((ti * 8 + q) * 16, 16), pl.ds(k * 256 + h * 128, 128)] = tile
    weights.wait()


def send_kernel(
    tab_in, lhs_in, lab, from_c, from_x, from_a, from_b, diff, bank, out,
    tab, lhs, prod, owns, pairs, sides, corners, sems,
):
    copies = [pltpu.make_async_copy(src, dst, sems.at[n]) for n, (src, dst) in enumerate(((tab_in, tab), (lhs_in, lhs)))]
    for copy in copies:
        copy.start()
    lane = lanes((8, 128))
    sub = lax.broadcasted_iota(jnp.int32, (8, 128), 0)
    a_of, b_of = lane // 16, lane % 16
    is_label = (a_of == 2) & (b_of >= 4) & (b_of < 12) | (a_of == 3) & (b_of >= 4) & (b_of < 6)
    absent = jnp.where(is_label, ABSENT, 0.0)
    offset = (sub - 1).astype(jnp.float32)

    zero = jnp.zeros((8, 128), jnp.float32)

    def clear(o, carry):
        at = pl.multiple_of(o * 16, 16)
        half = pl.multiple_of(o * 8, 8)
        owns[pl.ds(at, 8), :] = zero
        owns[pl.ds(at + 8, 8), :] = zero
        pairs[pl.ds(at, 8), :] = zero
        pairs[pl.ds(at + 8, 8), :] = zero
        sides[pl.ds(half, 8), :] = zero
        corners[pl.ds(at, 8), :] = zero
        corners[pl.ds(at + 8, 8), :] = zero
        return carry

    lax.fori_loop(0, OWNERS, clear, 0, unroll=4)
    for copy in copies:
        copy.wait()

    above, below, before, after = sides_of(from_c, from_x, from_a, from_b)
    lane16 = lanes((16, 128))

    def add(ti, q, k, h, lo, hi, what):
        rows_at, cols_at = pl.ds((ti * 8 + q) * 16, 16), pl.ds(k * 256 + h * 128, 128)
        if hi - lo == 8:
            none = jnp.zeros((8, 128), jnp.float32)
            what = jnp.concatenate([what, none] if lo == 0 else [none, what], axis=0)
        lhs[rows_at, cols_at] = (lhs[rows_at, cols_at].astype(jnp.float32) + what).astype(jnp.bfloat16)

    top, bottom = above(0, 16) * -0.5, below(0, 16) * 0.5
    for q in range(8):
        add(0, q, 1, 0, 0, 16, jnp.where(lane16 < 16, pltpu.roll(top, (128 - 16 * q) % 128, 1), 0.0))
        add(3, q, 1, 1, 0, 16, jnp.where(lane16 >= 112, pltpu.roll(bottom, 112 - 16 * q, 1), 0.0))
    left, right = before(0, 8) * -0.5, after(0, 8) * 0.5
    for ti in range(4):
        for h in range(2):
            low = jnp.zeros((8, 128), jnp.float32)
            high = jnp.zeros((8, 128), jnp.float32)
            for q in range(8):
                i = ti * 16 + h * 8 + q
                low = jnp.where(lane == q * 16, left[:, i : i + 1], low)
                high = jnp.where(lane == q * 16 + 15, right[:, i : i + 1], high)
            add(ti, 0, 2, h, 0, 8, low)
            add(ti, 7, 2, h, 8, 16, high)

    def product(n, carry):
        rhs = jnp.concatenate([bank[2 * n], bank[2 * n + 1]], axis=1)
        res = jnp.dot(lhs[...], rhs, preferred_element_type=jnp.float32)
        at = pl.multiple_of(n * 1024, 1024)
        prod[pl.ds(at, 512), :] = res[:, :128]
        prod[pl.ds(at + 512, 512), :] = res[:, 128:]
        return carry

    lax.fori_loop(0, NWB // 2, product, 0, unroll=4)

    half_of, quarter_of = lane // 64, b_of // 4
    code = half_of * 4 + quarter_of

    def rows(ref, at):
        return ref.at[pl.ds(pl.multiple_of(at, 8), 8), :]

    for r in range(RECS):
        value = rows(prod, tab[PROD, r])[...]
        rows(owns, tab[OWN, r])[...] = value
        pltpu.store(rows(pairs, tab[XROW, r]), value, mask=half_of == tab[KX, r])
        pltpu.store(rows(sides, tab[YROW, r]), pltpu.roll(value, tab[SHIFT, r], 1), mask=quarter_of == tab[YQ, r])
        pltpu.store(rows(corners, tab[CROW, r]), value, mask=code == tab[CC, r])

    for du, dv in CORNERS:
        first = 0 if du < 0 else 24
        cells = diff[first : first + 8, :]
        high = cells.astype(jnp.bfloat16).astype(jnp.float32)
        low = cells - high
        to = rows(corners, neighbour(du, dv) * 16)
        if dv < 0:
            pltpu.store(to, pltpu.roll(high, 4, 1), mask=(lane >= 4) & (lane < 8))
            pltpu.store(to, pltpu.roll(low, 8, 1), mask=(lane >= 8) & (lane < 12))
        else:
            pltpu.store(to, pltpu.roll(high, 124, 1), mask=(lane >= 120) & (lane < 124))
            pltpu.store(to, pltpu.roll(low, 120, 1), mask=(lane >= 116) & (lane < 120))

    def convert(o, carry):
        at = pl.multiple_of(o * 16, 16)
        half = pl.ds(pl.multiple_of(o * 8, 8), 8)
        found = jnp.broadcast_to(lab[pl.ds(o, 1), :], (8, 128))
        tags = jnp.where(found > 0, found + offset, absent)
        last = tags + (corners[pl.ds(at, 8), :] + corners[pl.ds(at + 8, 8), :])
        out[o, 0] = owns[pl.ds(at, 16), :].astype(jnp.bfloat16)
        out[o, 1] = pairs[pl.ds(at, 16), :].astype(jnp.bfloat16)
        out[o, 2] = jnp.concatenate([sides[half, :], last], axis=0).astype(jnp.bfloat16)
        return carry

    lax.fori_loop(0, OWNERS, convert, 0, unroll=8)


def ocean_kernel(recv, diff, from_c, from_x, from_a, from_b, out, onehot, dext, u0, u1):
    lane = lanes((8, 128))
    b_of = lane % 16
    K = OWNERS * 16
    own_in = recv[:, 0].reshape(K, 128)
    pair_in = recv[:, 1].reshape(K, 128)
    side_in = recv[:, 2].reshape(K, 128)

    pick_row = lax.broadcasted_iota(jnp.int32, (16, 128), 0)
    pick_lane = lanes((16, 128))
    label_lane = jnp.where(pick_row < 8, 36 + pick_row, 44 + pick_row)
    pick = ((label_lane == pick_lane) & (pick_row < 10)).astype(jnp.float32).astype(jnp.bfloat16)
    keys = lax.dot_general(pick, side_in, (((1,), (1,)), ((), ())), preferred_element_type=jnp.float32)
    early = pltpu.roll(keys, K - 8, 1)
    klane = lanes((8, K))
    sub = lax.broadcasted_iota(jnp.int32, (8, K), 0).astype(jnp.float32)
    late = (klane & 8) != 0

    def spread(rows, at):
        return jnp.broadcast_to(rows[at : at + 1, :], (8, K))

    def both(at):
        return jnp.where(late, spread(keys, at + 1), spread(early, at)) - sub

    def first(at):
        return jnp.where(late, -1000.0, spread(early, at)) - sub

    def hot(base, key, count):
        for t in range(0, count, 2):
            pair = [jnp.where(key == 8.0 * (t + q), 1.0, 0.0) for q in range(2)]
            onehot[pl.ds(base + t * 8, 16), :] = jnp.concatenate(pair, axis=0).astype(jnp.bfloat16)

    hot(0, both(0), 32)
    hot(256, both(2), 8)
    hot(320, both(4), 8)
    hot(384, first(6), 4)
    hot(416, first(7), 4)
    hot(448, first(8), 4)
    hot(480, first(9), 4)
    hot(512, jnp.where(late, (klane & 7).astype(jnp.float32), -1000.0) - sub, 2)

    def dot(lo, hi, rhs):
        return jnp.dot(onehot[lo:hi, :], rhs, preferred_element_type=jnp.float32)

    own = dot(0, 256, own_in)
    pairs = dot(256, 384, pair_in)
    sides = dot(384, 528, side_in)

    def tile(x, at):
        return x[at * 8 : at * 8 + 8, :]

    def put_side(cells, rows):
        for a, e in rows:
            right = pltpu.roll(cells, (128 - 16 * a) % 128, 1)
            left = pltpu.roll(cells, (112 - 16 * a) % 128, 1)
            u0[e, :, 128:256] = jnp.where(lane < 4, right, jnp.where(lane >= 124, left, 0.0))

    for tx in range(4):
        rows = swap_blocks([tile(own, tx * 8 + ty) for ty in range(8)])
        for a in range(8):
            u0[4 + tx * 8 + a, :, 0:128] = rows[a]
        r = tile(sides, tx) + pltpu.roll(tile(sides, 4 + tx), 124, 1)
        l = tile(sides, 8 + tx) + pltpu.roll(tile(sides, 12 + tx), 4, 1)
        put_side(jnp.where(b_of < 4, r, l), [(a, 4 + tx * 8 + a) for a in range(8)])
    rows = swap_blocks([tile(pairs, ty) for ty in range(8)])
    for a in range(4):
        u0[36 + a, :, 0:128] = rows[a]
    rows = swap_blocks([tile(pairs, 8 + ty) for ty in range(8)])
    for a in range(4, 8):
        u0[a - 4, :, 0:128] = rows[a]
    put_side(tile(sides, 16), [(a, 36 + a) for a in range(4)] + [(a, a - 4) for a in range(4, 8)])

    above, below, before, after = sides_of(from_c, from_x, from_a, from_b)

    def flag(du, dv):
        return jnp.where(neighbour(du, dv) < OWNERS, 1.0, 0.0)

    def corner(du, dv):
        s = neighbour(du, dv)
        z = recv[jnp.minimum(s, OWNERS - 1), 2].astype(jnp.float32)[8:16, :]
        z = jnp.where(s < OWNERS, z, 0.0)
        left = pltpu.roll(z, 4, 1) + pltpu.roll(z, 8, 1)
        right = pltpu.roll(z, 124, 1) + pltpu.roll(z, 120, 1)
        return left if dv < 0 else right

    def ends(left, right):
        return jnp.where(lane < 4, right, jnp.where(lane >= 124, left, 0.0))

    dext[0:8, 0:128] = above(40, 48) * flag(-1, 0)
    dext[40:48, 0:128] = below(16, 24) * flag(1, 0)
    dext[8:40, 0:128] = diff[...]
    dext[0:8, 128:256] = ends(corner(-1, -1), corner(-1, 1))
    dext[40:48, 128:256] = ends(corner(1, -1), corner(1, 1))
    for q in range(4):
        dext[8 + q * 8 : 16 + q * 8, 128:256] = ends(
            before(8 + q * 8, 16 + q * 8) * flag(0, -1), after(8 + q * 8, 16 + q * 8) * flag(0, 1)
        )

    src, dst = u0, u1
    for sweep in range(SWEEPS):
        for e in range(sweep + 1, 39 - sweep):
            u = src[e]
            beside = src[e + 1] + src[e - 1] + pltpu.roll(u, 255, 1) + pltpu.roll(u, 1, 1)
            d = jnp.broadcast_to(dext[e + 4 : e + 5, :], (8, 256))
            new = u + d * (beside - 4.0 * u)
            if sweep < SWEEPS - 1:
                dst[e] = new
            else:
                out[pl.ds(e - 4, 8, stride=OXD), :] = new[:, :128]
        src, dst = dst, src


def local(flux, diffusivity, remap_bank, rec_owner, rec_source, rec_target, rec_weight):
    vmem = pl.BlockSpec(memory_space=pltpu.VMEM)
    smem = pl.BlockSpec(memory_space=pltpu.SMEM)
    anywhere = pl.BlockSpec(memory_space=pl.ANY)
    flux_rows = flux.reshape(F * AXD, AYD)
    hbm = pl.BlockSpec(memory_space=pltpu.HBM)
    records = [x.reshape(1, RECS) for x in (rec_owner, rec_source, rec_target, rec_weight)]
    loads = [pltpu.with_memory_space_constraint(x, pltpu.HBM) for x in (flux_rows, diffusivity, *records)]
    f32, i32 = jnp.float32, jnp.int32
    to_c, to_x, to_a, to_b, tab, flux_halves, diff = pl.pallas_call(
        prepare_kernel,
        out_shape=[jax.ShapeDtypeStruct((48, 128), f32)] * 2
        + [jax.ShapeDtypeStruct((40, 128), f32)] * 2
        + [jax.ShapeDtypeStruct((TAB_ROWS, RECS), i32), jax.ShapeDtypeStruct((2, F * AXD, 128), f32)]
        + [jax.ShapeDtypeStruct((OXD, OYD), f32)],
        in_specs=[hbm] * 6,
        out_specs=[vmem] * 7,
        scratch_shapes=[pltpu.VMEM((4, 1, RECS), i32), pltpu.SemaphoreType.DMA((7,))],
        name="prepare",
        cost_estimate=pl.CostEstimate(flops=3000000000, bytes_accessed=8000000, transcendentals=0),
        compiler_params=pltpu.CompilerParams(vmem_limit_bytes=6 << 20),
    )(*loads)

    def swap(x, axis, count, odd):
        return lax.ppermute(x, axis, [(i, (((i + odd) ^ 1) - odd) % count) for i in range(count)])

    came = []
    for x, axis, count, odd in ((to_c, "gx", NGX, 0), (to_x, "gx", NGX, 1), (to_a, "gy", NGY, 0), (to_b, "gy", NGY, 1)):
        came.append(swap(x, axis, count, odd))

    bf16 = jnp.bfloat16
    lhs, lab, bank = pl.pallas_call(
        tiles_kernel,
        out_shape=[jax.ShapeDtypeStruct((512, 768), bf16), jax.ShapeDtypeStruct((OWNERS, 128), f32)]
        + [jax.ShapeDtypeStruct((NWB, 768, 128), bf16)],
        in_specs=[vmem, vmem, hbm],
        out_specs=[vmem] * 3,
        scratch_shapes=[pltpu.SemaphoreType.DMA],
        name="tiles",
    cost_estimate=pl.CostEstimate(flops=3000000000, bytes_accessed=8000000, transcendentals=0),
    compiler_params=pltpu.CompilerParams(vmem_limit_bytes=8 << 20),
    )(flux_halves, tab, remap_bank.reshape(NWB, 768, 128))

    outgoing = pl.pallas_call(
        send_kernel,
        out_shape=jax.ShapeDtypeStruct((OWNERS, 3, 16, 128), bf16),
        in_specs=[anywhere] * 2 + [vmem] * 7,
        out_specs=vmem,
        scratch_shapes=[
            pltpu.SMEM((TAB_ROWS, RECS), i32),
            pltpu.VMEM((512, 768), bf16),
            pltpu.VMEM((NWB * 512, 128), f32),
            pltpu.VMEM((OWNERS * 16, 128), f32),
            pltpu.VMEM((OWNERS * 16 + 16, 128), f32),
            pltpu.VMEM((OWNERS * 8 + 8, 128), f32),
            pltpu.VMEM((OWNERS * 16 + 16, 128), f32),
            pltpu.SemaphoreType.DMA((2,)),
        ],
        name="remap_send",
        cost_estimate=pl.CostEstimate(flops=5000000000, bytes_accessed=8000000, transcendentals=0),
        compiler_params=pltpu.CompilerParams(vmem_limit_bytes=24 << 20),
    )(tab, lhs, lab, *came, diff, bank)
    arrived = lax.all_to_all(outgoing, ("gx", "gy"), split_axis=0, concat_axis=0, tiled=True)
    ocean = pl.pallas_call(
        ocean_kernel,
        out_shape=jax.ShapeDtypeStruct((F * OXD, OYD), f32),
        in_specs=[vmem] * 6,
        out_specs=vmem,
        scratch_shapes=[
            pltpu.VMEM((528, OWNERS * 16), jnp.bfloat16),
            pltpu.VMEM((48, 256), f32),
            pltpu.VMEM((40, 8, 256), f32),
            pltpu.VMEM((40, 8, 256), f32),
        ],
        name="ocean",
        cost_estimate=pl.CostEstimate(flops=3000000000, bytes_accessed=4000000, transcendentals=0),
        compiler_params=pltpu.CompilerParams(vmem_limit_bytes=16 << 20),
    )(arrived, diff, *came)
    return ocean.reshape(F, OXD, OYD)


def solution(mesh):
    in_specs = (
        P(None, "gx", "gy"),
        P("gx", "gy"),
        P(),
        P(("gx", "gy")),
        P(("gx", "gy")),
        P(("gx", "gy")),
        P(("gx", "gy")),
    )
    return jax.shard_map(local, mesh=mesh, in_specs=in_specs, out_specs=P(None, "gx", "gy"), check_vma=False)
```

```python
import jax
import jax.numpy as jnp
from jax import lax
from jax.experimental import pallas as pl
from jax.experimental.pallas import tpu as pltpu
from jax.sharding import PartitionSpec as P


F = 8
AXD, AYD = 64, 256
OXD, OYD = 32, 128
NWB = 16
RECS = 128
SWEEPS = 4
OWNERS = 128
NGX, NGY = 8, 16
(PROD, OWN, XROW, YROW, CROW, KX, YQ, CC, SHIFT, OWNER, XTO, YTO, PO, PX, PY, VO, VX, VY) = range(18)
TAB_ROWS = 24
ABSENT = 256.0
CORNERS = ((-1, -1), (-1, 1), (1, -1), (1, 1))


def lanes(shape):
    return lax.broadcasted_iota(jnp.int32, shape, 1)


def swap_blocks(v):
    block = lanes(v[0].shape) // 16
    for s in range(3):
        d = 1 << s
        high = (block & d) != 0
        n = list(v)
        for p in range(8):
            if not p & d:
                a, b = v[p], v[p | d]
                if d == 4:
                    up = down = pltpu.roll(jnp.where(high, a, b), 64, 1)
                else:
                    up, down = pltpu.roll(b, 16 * d, 1), pltpu.roll(a, 128 - 16 * d, 1)
                n[p] = jnp.where(high, up, a)
                n[p | d] = jnp.where(high, b, down)
        v = n
    return v


def neighbour(du, dv):
    gx, gy = lax.axis_index("gx") + du, lax.axis_index("gy") + dv
    return jnp.where((gx >= 0) & (gx < NGX) & (gy >= 0) & (gy < NGY), gx * NGY + gy, OWNERS)


def even(axis):
    return lax.axis_index(axis) % 2 == 0


def sides_of(from_c, from_x, from_a, from_b):
    even_x, even_y = even("gx"), even("gy")
    return (
        lambda lo, hi: jnp.where(even_x, from_x[lo:hi, :], from_c[lo:hi, :]),
        lambda lo, hi: jnp.where(even_x, from_c[lo:hi, :], from_x[lo:hi, :]),
        lambda lo, hi: jnp.where(even_y, from_b[lo:hi, :], from_a[lo:hi, :]),
        lambda lo, hi: jnp.where(even_y, from_a[lo:hi, :], from_b[lo:hi, :]),
    )


def prepare_kernel(flux_in, diff_in, owner_in, source_in, target_in, weight_in, to_c, to_x, to_a, to_b, tab, flux, diff, ids, sems):
    moves = [(x, ids.at[n]) for n, x in enumerate((owner_in, source_in, target_in, weight_in))]
    moves += [(diff_in, diff)] + [(flux_in.at[:, pl.ds(g * 128, 128)], flux.at[g]) for g in range(2)]
    copies = [pltpu.make_async_copy(src, dst, sems.at[n]) for n, (src, dst) in enumerate(moves)]
    for copy in copies:
        copy.start()
    lane = lanes((8, 128))
    for copy in copies[:5]:
        copy.wait()
    owner, source, target, weight = (ids[n] for n in range(4))
    across = jnp.broadcast_to(owner, (RECS, RECS))
    along = jnp.transpose(across.astype(jnp.float32)).astype(jnp.int32)
    sub = lax.broadcasted_iota(jnp.int32, (RECS, RECS), 0)
    earlier = jnp.where((across == along) & (sub < lanes((RECS, RECS))), 1.0, 0.0)
    slot = jnp.sum(earlier, axis=0, keepdims=True).astype(jnp.int32)
    ox, oy = owner >> 4, owner & 15
    tx, ty = target >> 3, target & 7
    sx = jnp.where(tx == 0, -1, jnp.where(tx == 3, 1, 0))
    sy = jnp.where(ty == 0, -1, jnp.where(ty == 7, 1, 0))
    ok_x = (sx != 0) & (ox + sx >= 0) & (ox + sx < NGX)
    ok_y = (sy != 0) & (oy + sy >= 0) & (oy + sy < NGY)
    dx = jnp.where(ok_x, owner + sx * NGY, OWNERS)
    dy = jnp.where(ok_y, owner + sy, OWNERS)
    dc = jnp.where(ok_x & ok_y, owner + sx * NGY + sy, OWNERS)
    kx = jnp.where(tx == 3, 1, 0)
    ky = jnp.where(ty == 7, 1, 0)
    ti, tj = source >> 4, source & 15
    t8 = (ti * 16 + (tj & 7) * 2 + (tj >> 3)) * 8
    rows = [
        weight * 512 + t8, owner * 16 + slot * 8, dx * 16 + slot * 8, dy * 8, dc * 16 + slot * 8,
        kx, jnp.where(ky == 0, slot, 3 - slot), kx * 4 + ky * 3, jnp.where(ky == 0, 4 * slot, (128 - 4 * slot) & 127),
        owner, dx, dy, 36 + slot, 38 + 2 * kx + slot, jnp.where(ky == 0, 42, 52) + slot,
        target * 8 + 1, ty * 8 + 1, tx * 8 + 1,
    ]
    for n, value in enumerate(rows):
        tab[n : n + 1, :] = value
    for n in range(len(rows), TAB_ROWS):
        tab[n : n + 1, :] = slot

    for to in (to_c, to_x):
        to[16:48, :] = diff[...]
    for to in (to_a, to_b):
        to[8:40, :] = diff[...]
    for copy in copies[5:]:
        copy.wait()

    def row(i, g):
        return flux[g, pl.ds(i, 8, stride=AXD), :]

    even_x, even_y = even("gx"), even("gy")
    for g in range(2):
        bottom, top = row(AXD - 1, g), row(0, g)
        to_c[g * 8 : g * 8 + 8, :] = jnp.where(even_x, bottom, top)
        to_x[g * 8 : g * 8 + 8, :] = jnp.where(even_x, top, bottom)
    last = jnp.zeros((8, 128), jnp.float32)
    first = jnp.zeros((8, 128), jnp.float32)
    for i in range(AXD):
        last = jnp.where(lane == i, row(i, 1)[:, 127:128], last)
        first = jnp.where(lane == i, row(i, 0)[:, 0:1], first)
    to_a[0:8, :] = jnp.where(even_y, last, first)
    to_b[0:8, :] = jnp.where(even_y, first, last)


def tiles_kernel(flux, tabv, lhs, lab):
    rows3 = lax.broadcasted_iota(jnp.int32, (128, 3 * RECS), 0)

    def three(*at):
        return jnp.concatenate([jnp.broadcast_to(tabv[n : n + 1, :], (128, RECS)) for n in at], axis=1)

    going = jnp.where(three(OWNER, XTO, YTO) == rows3, 1.0, 0.0).astype(jnp.bfloat16)
    label = jnp.where(three(PO, PX, PY) == rows3, three(VO, VX, VY), 0).astype(jnp.float32).astype(jnp.bfloat16)
    lab[...] = lax.dot_general(going, label, (((1,), (1,)), ((), ())), preferred_element_type=jnp.float32)

    wide = lanes((8, 256))
    outside = jnp.zeros((8, 256), jnp.float32)

    def row(i):
        if i < 0 or i >= AXD:
            return outside
        return jnp.concatenate([flux[g, pl.ds(i, 8, stride=AXD), :] for g in range(2)], axis=1)

    for ti in range(4):
        x = [row(i) for i in range(ti * 16 - 1, ti * 16 + 17)]
        for k in range(3):
            vals = []
            for a in range(16):
                if k == 0:
                    vals.append(x[a + 1])
                elif k == 1:
                    vals.append((x[a + 2] - x[a]) * 0.5)
                else:
                    nxt = jnp.where(wide == 255, 0.0, pltpu.roll(x[a + 1], 255, 1))
                    prv = jnp.where(wide == 0, 0.0, pltpu.roll(x[a + 1], 1, 1))
                    vals.append((nxt - prv) * 0.5)
            for h in range(2):
                packed = [
                    jnp.concatenate([vals[h * 8 + q][:, :128], vals[h * 8 + q][:, 128:]], axis=0).astype(jnp.bfloat16)
                    for q in range(8)
                ]
                for q, tile in enumerate(swap_blocks(packed)):
                    lhs[pl.ds((ti * 8 + q) * 16, 16), pl.ds(k * 256 + h * 128, 128)] = tile


def send_kernel(
    tab_in, lhs_in, lab, from_c, from_x, from_a, from_b, diff, bank, out,
    tab, lhs, prod, owns, pairs, sides, corners, sems,
):
    copies = [pltpu.make_async_copy(src, dst, sems.at[n]) for n, (src, dst) in enumerate(((tab_in, tab), (lhs_in, lhs)))]
    for copy in copies:
        copy.start()
    lane = lanes((8, 128))
    sub = lax.broadcasted_iota(jnp.int32, (8, 128), 0)
    a_of, b_of = lane // 16, lane % 16
    is_label = (a_of == 2) & (b_of >= 4) & (b_of < 12) | (a_of == 3) & (b_of >= 4) & (b_of < 6)
    absent = jnp.where(is_label, ABSENT, 0.0)
    offset = (sub - 1).astype(jnp.float32)

    zero = jnp.zeros((8, 128), jnp.float32)

    def clear(o, carry):
        at = pl.multiple_of(o * 16, 16)
        half = pl.multiple_of(o * 8, 8)
        owns[pl.ds(at, 8), :] = zero
        owns[pl.ds(at + 8, 8), :] = zero
        pairs[pl.ds(at, 8), :] = zero
        pairs[pl.ds(at + 8, 8), :] = zero
        sides[pl.ds(half, 8), :] = zero
        corners[pl.ds(at, 8), :] = zero
        corners[pl.ds(at + 8, 8), :] = zero
        return carry

    lax.fori_loop(0, OWNERS, clear, 0, unroll=4)
    for copy in copies:
        copy.wait()

    above, below, before, after = sides_of(from_c, from_x, from_a, from_b)
    lane16 = lanes((16, 128))

    def add(ti, q, k, h, lo, hi, what):
        rows_at, cols_at = pl.ds((ti * 8 + q) * 16, 16), pl.ds(k * 256 + h * 128, 128)
        if hi - lo == 8:
            none = jnp.zeros((8, 128), jnp.float32)
            what = jnp.concatenate([what, none] if lo == 0 else [none, what], axis=0)
        lhs[rows_at, cols_at] = (lhs[rows_at, cols_at].astype(jnp.float32) + what).astype(jnp.bfloat16)

    top, bottom = above(0, 16) * -0.5, below(0, 16) * 0.5
    for q in range(8):
        add(0, q, 1, 0, 0, 16, jnp.where(lane16 < 16, pltpu.roll(top, (128 - 16 * q) % 128, 1), 0.0))
        add(3, q, 1, 1, 0, 16, jnp.where(lane16 >= 112, pltpu.roll(bottom, 112 - 16 * q, 1), 0.0))
    left, right = before(0, 8) * -0.5, after(0, 8) * 0.5
    for ti in range(4):
        for h in range(2):
            low = jnp.zeros((8, 128), jnp.float32)
            high = jnp.zeros((8, 128), jnp.float32)
            for q in range(8):
                i = ti * 16 + h * 8 + q
                low = jnp.where(lane == q * 16, left[:, i : i + 1], low)
                high = jnp.where(lane == q * 16 + 15, right[:, i : i + 1], high)
            add(ti, 0, 2, h, 0, 8, low)
            add(ti, 7, 2, h, 8, 16, high)

    def product(n, carry):
        rhs = jnp.concatenate([bank[2 * n], bank[2 * n + 1]], axis=1)
        res = jnp.dot(lhs[...], rhs, preferred_element_type=jnp.float32)
        at = pl.multiple_of(n * 1024, 1024)
        prod[pl.ds(at, 512), :] = res[:, :128]
        prod[pl.ds(at + 512, 512), :] = res[:, 128:]
        return carry

    lax.fori_loop(0, NWB // 2, product, 0, unroll=8)

    half_of, quarter_of = lane // 64, b_of // 4
    code = half_of * 4 + quarter_of

    def rows(ref, at):
        return ref.at[pl.ds(pl.multiple_of(at, 8), 8), :]

    for r in range(RECS):
        value = rows(prod, tab[PROD, r])[...]
        rows(owns, tab[OWN, r])[...] = value
        pltpu.store(rows(pairs, tab[XROW, r]), value, mask=half_of == tab[KX, r])
        pltpu.store(rows(sides, tab[YROW, r]), pltpu.roll(value, tab[SHIFT, r], 1), mask=quarter_of == tab[YQ, r])
        pltpu.store(rows(corners, tab[CROW, r]), value, mask=code == tab[CC, r])

    for du, dv in CORNERS:
        first = 0 if du < 0 else 24
        cells = diff[first : first + 8, :]
        high = cells.astype(jnp.bfloat16).astype(jnp.float32)
        low = cells - high
        to = rows(corners, neighbour(du, dv) * 16)
        if dv < 0:
            pltpu.store(to, pltpu.roll(high, 4, 1), mask=(lane >= 4) & (lane < 8))
            pltpu.store(to, pltpu.roll(low, 8, 1), mask=(lane >= 8) & (lane < 12))
        else:
            pltpu.store(to, pltpu.roll(high, 124, 1), mask=(lane >= 120) & (lane < 124))
            pltpu.store(to, pltpu.roll(low, 120, 1), mask=(lane >= 116) & (lane < 120))

    def convert(o, carry):
        at = pl.multiple_of(o * 16, 16)
        half = pl.ds(pl.multiple_of(o * 8, 8), 8)
        found = jnp.broadcast_to(lab[pl.ds(o, 1), :], (8, 128))
        tags = jnp.where(found > 0, found + offset, absent)
        last = tags + (corners[pl.ds(at, 8), :] + corners[pl.ds(at + 8, 8), :])
        out[o, 0] = owns[pl.ds(at, 16), :].astype(jnp.bfloat16)
        out[o, 1] = pairs[pl.ds(at, 16), :].astype(jnp.bfloat16)
        out[o, 2] = jnp.concatenate([sides[half, :], last], axis=0).astype(jnp.bfloat16)
        return carry

    lax.fori_loop(0, OWNERS, convert, 0, unroll=8)


def ocean_kernel(recv, diff, from_c, from_x, from_a, from_b, out, onehot, dext, u0, u1):
    lane = lanes((8, 128))
    b_of = lane % 16
    K = OWNERS * 16
    own_in = recv[:, 0].reshape(K, 128)
    pair_in = recv[:, 1].reshape(K, 128)
    side_in = recv[:, 2].reshape(K, 128)

    pick_row = lax.broadcasted_iota(jnp.int32, (16, 128), 0)
    pick_lane = lanes((16, 128))
    label_lane = jnp.where(pick_row < 8, 36 + pick_row, 44 + pick_row)
    pick = ((label_lane == pick_lane) & (pick_row < 10)).astype(jnp.float32).astype(jnp.bfloat16)
    keys = lax.dot_general(pick, side_in, (((1,), (1,)), ((), ())), preferred_element_type=jnp.float32)
    early = pltpu.roll(keys, K - 8, 1)
    klane = lanes((8, K))
    sub = lax.broadcasted_iota(jnp.int32, (8, K), 0).astype(jnp.float32)
    late = (klane & 8) != 0

    def spread(rows, at):
        return jnp.broadcast_to(rows[at : at + 1, :], (8, K))

    def both(at):
        return jnp.where(late, spread(keys, at + 1), spread(early, at)) - sub

    def first(at):
        return jnp.where(late, -1000.0, spread(early, at)) - sub

    def hot(base, key, count):
        for t in range(0, count, 2):
            pair = [jnp.where(key == 8.0 * (t + q), 1.0, 0.0) for q in range(2)]
            onehot[pl.ds(base + t * 8, 16), :] = jnp.concatenate(pair, axis=0).astype(jnp.bfloat16)

    hot(0, both(0), 32)
    hot(256, both(2), 8)
    hot(320, both(4), 8)
    hot(384, first(6), 4)
    hot(416, first(7), 4)
    hot(448, first(8), 4)
    hot(480, first(9), 4)
    hot(512, jnp.where(late, (klane & 7).astype(jnp.float32), -1000.0) - sub, 2)

    def dot(lo, hi, rhs):
        return jnp.dot(onehot[lo:hi, :], rhs, preferred_element_type=jnp.float32)

    own = dot(0, 256, own_in)
    pairs = dot(256, 384, pair_in)
    sides = dot(384, 528, side_in)

    def tile(x, at):
        return x[at * 8 : at * 8 + 8, :]

    def put_side(cells, rows):
        for a, e in rows:
            right = pltpu.roll(cells, (128 - 16 * a) % 128, 1)
            left = pltpu.roll(cells, (112 - 16 * a) % 128, 1)
            u0[e, :, 128:256] = jnp.where(lane < 4, right, jnp.where(lane >= 124, left, 0.0))

    for tx in range(4):
        rows = swap_blocks([tile(own, tx * 8 + ty) for ty in range(8)])
        for a in range(8):
            u0[4 + tx * 8 + a, :, 0:128] = rows[a]
        r = tile(sides, tx) + pltpu.roll(tile(sides, 4 + tx), 124, 1)
        l = tile(sides, 8 + tx) + pltpu.roll(tile(sides, 12 + tx), 4, 1)
        put_side(jnp.where(b_of < 4, r, l), [(a, 4 + tx * 8 + a) for a in range(8)])
    rows = swap_blocks([tile(pairs, ty) for ty in range(8)])
    for a in range(4):
        u0[36 + a, :, 0:128] = rows[a]
    rows = swap_blocks([tile(pairs, 8 + ty) for ty in range(8)])
    for a in range(4, 8):
        u0[a - 4, :, 0:128] = rows[a]
    put_side(tile(sides, 16), [(a, 36 + a) for a in range(4)] + [(a, a - 4) for a in range(4, 8)])

    above, below, before, after = sides_of(from_c, from_x, from_a, from_b)

    def flag(du, dv):
        return jnp.where(neighbour(du, dv) < OWNERS, 1.0, 0.0)

    def corner(du, dv):
        s = neighbour(du, dv)
        z = recv[jnp.minimum(s, OWNERS - 1), 2].astype(jnp.float32)[8:16, :]
        z = jnp.where(s < OWNERS, z, 0.0)
        left = pltpu.roll(z, 4, 1) + pltpu.roll(z, 8, 1)
        right = pltpu.roll(z, 124, 1) + pltpu.roll(z, 120, 1)
        return left if dv < 0 else right

    def ends(left, right):
        return jnp.where(lane < 4, right, jnp.where(lane >= 124, left, 0.0))

    dext[0:8, 0:128] = above(40, 48) * flag(-1, 0)
    dext[40:48, 0:128] = below(16, 24) * flag(1, 0)
    dext[8:40, 0:128] = diff[...]
    dext[0:8, 128:256] = ends(corner(-1, -1), corner(-1, 1))
    dext[40:48, 128:256] = ends(corner(1, -1), corner(1, 1))
    for q in range(4):
        dext[8 + q * 8 : 16 + q * 8, 128:256] = ends(
            before(8 + q * 8, 16 + q * 8) * flag(0, -1), after(8 + q * 8, 16 + q * 8) * flag(0, 1)
        )

    src, dst = u0, u1
    for sweep in range(SWEEPS):
        for e in range(sweep + 1, 39 - sweep):
            u = src[e]
            beside = src[e + 1] + src[e - 1] + pltpu.roll(u, 255, 1) + pltpu.roll(u, 1, 1)
            d = jnp.broadcast_to(dext[e + 4 : e + 5, :], (8, 256))
            new = u + d * (beside - 4.0 * u)
            if sweep < SWEEPS - 1:
                dst[e] = new
            else:
                out[pl.ds(e - 4, 8, stride=OXD), :] = new[:, :128]
        src, dst = dst, src


def local(flux, diffusivity, remap_bank, rec_owner, rec_source, rec_target, rec_weight):
    vmem = pl.BlockSpec(memory_space=pltpu.VMEM)
    smem = pl.BlockSpec(memory_space=pltpu.SMEM)
    anywhere = pl.BlockSpec(memory_space=pl.ANY)
    flux_rows = flux.reshape(F * AXD, AYD)
    hbm = pl.BlockSpec(memory_space=pltpu.HBM)
    records = [x.reshape(1, RECS) for x in (rec_owner, rec_source, rec_target, rec_weight)]
    loads = [pltpu.with_memory_space_constraint(x, pltpu.HBM) for x in (flux_rows, diffusivity, *records)]
    f32, i32 = jnp.float32, jnp.int32
    to_c, to_x, to_a, to_b, tab, flux_halves, diff = pl.pallas_call(
        prepare_kernel,
        out_shape=[jax.ShapeDtypeStruct((48, 128), f32)] * 2
        + [jax.ShapeDtypeStruct((40, 128), f32)] * 2
        + [jax.ShapeDtypeStruct((TAB_ROWS, RECS), i32), jax.ShapeDtypeStruct((2, F * AXD, 128), f32)]
        + [jax.ShapeDtypeStruct((OXD, OYD), f32)],
        in_specs=[hbm] * 6,
        out_specs=[vmem] * 7,
        scratch_shapes=[pltpu.VMEM((4, 1, RECS), i32), pltpu.SemaphoreType.DMA((7,))],
        name="prepare",
        cost_estimate=pl.CostEstimate(flops=3000000000, bytes_accessed=8000000, transcendentals=0),
        compiler_params=pltpu.CompilerParams(vmem_limit_bytes=6 << 20),
    )(*loads)

    def swap(x, axis, count, odd):
        return lax.ppermute(x, axis, [(i, (((i + odd) ^ 1) - odd) % count) for i in range(count)])

    came = []
    for x, axis, count, odd in ((to_c, "gx", NGX, 0), (to_x, "gx", NGX, 1), (to_a, "gy", NGY, 0), (to_b, "gy", NGY, 1)):
        came.append(swap(x, axis, count, odd))

    bf16 = jnp.bfloat16
    lhs, lab = pl.pallas_call(
        tiles_kernel,
        out_shape=[jax.ShapeDtypeStruct((512, 768), bf16), jax.ShapeDtypeStruct((OWNERS, 128), f32)],
        in_specs=[vmem] * 2,
        out_specs=[vmem] * 2,
        name="tiles",
    cost_estimate=pl.CostEstimate(flops=3000000000, bytes_accessed=8000000, transcendentals=0),
    compiler_params=pltpu.CompilerParams(vmem_limit_bytes=8 << 20),
    )(flux_halves, tab)

    outgoing = pl.pallas_call(
        send_kernel,
        out_shape=jax.ShapeDtypeStruct((OWNERS, 3, 16, 128), bf16),
        in_specs=[anywhere] * 2 + [vmem] * 7,
        out_specs=vmem,
        scratch_shapes=[
            pltpu.SMEM((TAB_ROWS, RECS), i32),
            pltpu.VMEM((512, 768), bf16),
            pltpu.VMEM((NWB * 512, 128), f32),
            pltpu.VMEM((OWNERS * 16, 128), f32),
            pltpu.VMEM((OWNERS * 16 + 16, 128), f32),
            pltpu.VMEM((OWNERS * 8 + 8, 128), f32),
            pltpu.VMEM((OWNERS * 16 + 16, 128), f32),
            pltpu.SemaphoreType.DMA((2,)),
        ],
        name="remap_send",
        cost_estimate=pl.CostEstimate(flops=5000000000, bytes_accessed=8000000, transcendentals=0),
        compiler_params=pltpu.CompilerParams(vmem_limit_bytes=24 << 20),
    )(tab, lhs, lab, *came, diff, remap_bank.reshape(NWB, 768, 128))
    arrived = lax.all_to_all(outgoing, ("gx", "gy"), split_axis=0, concat_axis=0, tiled=True)
    ocean = pl.pallas_call(
        ocean_kernel,
        out_shape=jax.ShapeDtypeStruct((F * OXD, OYD), f32),
        in_specs=[vmem] * 6,
        out_specs=vmem,
        scratch_shapes=[
            pltpu.VMEM((528, OWNERS * 16), jnp.bfloat16),
            pltpu.VMEM((48, 256), f32),
            pltpu.VMEM((40, 8, 256), f32),
            pltpu.VMEM((40, 8, 256), f32),
        ],
        name="ocean",
        cost_estimate=pl.CostEstimate(flops=3000000000, bytes_accessed=4000000, transcendentals=0),
        compiler_params=pltpu.CompilerParams(vmem_limit_bytes=16 << 20),
    )(arrived, diff, *came)
    return ocean.reshape(F, OXD, OYD)


def solution(mesh):
    in_specs = (
        P(None, "gx", "gy"),
        P("gx", "gy"),
        P(),
        P(("gx", "gy")),
        P(("gx", "gy")),
        P(("gx", "gy")),
        P(("gx", "gy")),
    )
    return jax.shard_map(local, mesh=mesh, in_specs=in_specs, out_specs=P(None, "gx", "gy"), check_vma=False)
```

```python
import jax
import jax.numpy as jnp
from jax import lax
from jax.experimental import pallas as pl
from jax.experimental.pallas import tpu as pltpu
from jax.sharding import PartitionSpec as P


F = 8
AXD, AYD = 64, 256
OXD, OYD = 32, 128
NWB = 16
RECS = 128
SWEEPS = 4
OWNERS = 128
NGX, NGY = 8, 16
(PROD, OWN, XROW, YROW, CROW, KX, YQ, CC, SHIFT, OWNER, XTO, YTO, PO, PX, PY, VO, VX, VY, XTURN) = range(19)
TAB_ROWS = 24
ABSENT = 256.0
CORNERS = ((-1, -1), (-1, 1), (1, -1), (1, 1))


def lanes(shape):
    return lax.broadcasted_iota(jnp.int32, shape, 1)


def swap_blocks(v):
    block = lanes(v[0].shape) // 16
    for s in range(3):
        d = 1 << s
        high = (block & d) != 0
        n = list(v)
        for p in range(8):
            if not p & d:
                a, b = v[p], v[p | d]
                if d == 4:
                    up = down = pltpu.roll(jnp.where(high, a, b), 64, 1)
                else:
                    up, down = pltpu.roll(b, 16 * d, 1), pltpu.roll(a, 128 - 16 * d, 1)
                n[p] = jnp.where(high, up, a)
                n[p | d] = jnp.where(high, b, down)
        v = n
    return v


def neighbour(du, dv):
    gx, gy = lax.axis_index("gx") + du, lax.axis_index("gy") + dv
    return jnp.where((gx >= 0) & (gx < NGX) & (gy >= 0) & (gy < NGY), gx * NGY + gy, OWNERS)


def even(axis):
    return lax.axis_index(axis) % 2 == 0


def sides_of(from_c, from_x, from_a, from_b):
    even_x, even_y = even("gx"), even("gy")
    return (
        lambda lo, hi: jnp.where(even_x, from_x[lo:hi, :], from_c[lo:hi, :]),
        lambda lo, hi: jnp.where(even_x, from_c[lo:hi, :], from_x[lo:hi, :]),
        lambda lo, hi: jnp.where(even_y, from_b[lo:hi, :], from_a[lo:hi, :]),
        lambda lo, hi: jnp.where(even_y, from_a[lo:hi, :], from_b[lo:hi, :]),
    )


def prepare_kernel(flux_in, diff_in, owner_in, source_in, target_in, weight_in, to_c, to_x, to_a, to_b, tab, flux, diff, ids, sems):
    moves = [(x, ids.at[n]) for n, x in enumerate((owner_in, source_in, target_in, weight_in))]
    moves += [(diff_in, diff)] + [(flux_in.at[:, pl.ds(g * 128, 128)], flux.at[g]) for g in range(2)]
    copies = [pltpu.make_async_copy(src, dst, sems.at[n]) for n, (src, dst) in enumerate(moves)]
    for copy in copies:
        copy.start()
    lane = lanes((8, 128))
    for copy in copies[:5]:
        copy.wait()
    owner, source, target, weight = (ids[n] for n in range(4))
    across = jnp.broadcast_to(owner, (RECS, RECS))
    along = jnp.transpose(across.astype(jnp.float32)).astype(jnp.int32)
    sub = lax.broadcasted_iota(jnp.int32, (RECS, RECS), 0)
    earlier = jnp.where((across == along) & (sub < lanes((RECS, RECS))), 1.0, 0.0)
    slot = jnp.sum(earlier, axis=0, keepdims=True).astype(jnp.int32)
    ox, oy = owner >> 4, owner & 15
    tx, ty = target >> 3, target & 7
    sx = jnp.where(tx == 0, -1, jnp.where(tx == 3, 1, 0))
    sy = jnp.where(ty == 0, -1, jnp.where(ty == 7, 1, 0))
    odd_x = ox & 1
    ok_x = (sx == -1) & (odd_x == 0) & (ox > 0) | (sx == 1) & (odd_x == 1) & (ox < NGX - 1)
    ok_y = (sy != 0) & (oy + sy >= 0) & (oy + sy < NGY)
    dx = jnp.where(ok_x, owner + sx * NGY, OWNERS)
    dy = jnp.where(ok_y, owner + sy, OWNERS)
    dc = jnp.where(ok_x & ok_y, owner + sx * NGY + sy, OWNERS)
    kx = jnp.where(tx == 3, 1, 0)
    ky = jnp.where(ty == 7, 1, 0)
    ti, tj = source >> 4, source & 15
    t8 = (ti * 16 + (tj & 7) * 2 + (tj >> 3)) * 8
    rows = [
        weight * 512 + t8, owner * 16 + slot * 8, dx * 8, dy * 8, dc * 16 + slot * 8,
        (kx + slot) & 1, jnp.where(ky == 0, slot, 3 - slot), kx * 4 + ky * 3, jnp.where(ky == 0, 4 * slot, (128 - 4 * slot) & 127),
        owner, dx, dy, 36 + slot, 38 + 2 * kx + slot, jnp.where(ky == 0, 42, 52) + slot,
        target * 8 + 1, ty * 8 + 1, tx * 8 + 1, slot * 64,
    ]
    for n, value in enumerate(rows):
        tab[n : n + 1, :] = value
    for n in range(len(rows), TAB_ROWS):
        tab[n : n + 1, :] = slot

    for to in (to_c, to_x):
        to[16:48, :] = diff[...]
    for to in (to_a, to_b):
        to[8:40, :] = diff[...]
    for copy in copies[5:]:
        copy.wait()

    def row(i, g):
        return flux[g, pl.ds(i, 8, stride=AXD), :]

    even_x, even_y = even("gx"), even("gy")
    for g in range(2):
        bottom, top = row(AXD - 1, g), row(0, g)
        to_c[g * 8 : g * 8 + 8, :] = jnp.where(even_x, bottom, top)
        to_x[g * 8 : g * 8 + 8, :] = jnp.where(even_x, top, bottom)
    last = jnp.zeros((8, 128), jnp.float32)
    first = jnp.zeros((8, 128), jnp.float32)
    for i in range(AXD):
        last = jnp.where(lane == i, row(i, 1)[:, 127:128], last)
        first = jnp.where(lane == i, row(i, 0)[:, 0:1], first)
    to_a[0:8, :] = jnp.where(even_y, last, first)
    to_b[0:8, :] = jnp.where(even_y, first, last)


def tiles_kernel(flux, tabv, lhs, lab):
    rows3 = lax.broadcasted_iota(jnp.int32, (128, 3 * RECS), 0)

    def three(*at):
        return jnp.concatenate([jnp.broadcast_to(tabv[n : n + 1, :], (128, RECS)) for n in at], axis=1)

    going = jnp.where(three(OWNER, XTO, YTO) == rows3, 1.0, 0.0).astype(jnp.bfloat16)
    label = jnp.where(three(PO, PX, PY) == rows3, three(VO, VX, VY), 0).astype(jnp.float32).astype(jnp.bfloat16)
    lab[...] = lax.dot_general(going, label, (((1,), (1,)), ((), ())), preferred_element_type=jnp.float32)

    wide = lanes((8, 256))
    outside = jnp.zeros((8, 256), jnp.float32)

    def row(i):
        if i < 0 or i >= AXD:
            return outside
        return jnp.concatenate([flux[g, pl.ds(i, 8, stride=AXD), :] for g in range(2)], axis=1)

    for ti in range(4):
        x = [row(i) for i in range(ti * 16 - 1, ti * 16 + 17)]
        for k in range(3):
            vals = []
            for a in range(16):
                if k == 0:
                    vals.append(x[a + 1])
                elif k == 1:
                    vals.append((x[a + 2] - x[a]) * 0.5)
                else:
                    nxt = jnp.where(wide == 255, 0.0, pltpu.roll(x[a + 1], 255, 1))
                    prv = jnp.where(wide == 0, 0.0, pltpu.roll(x[a + 1], 1, 1))
                    vals.append((nxt - prv) * 0.5)
            for h in range(2):
                packed = [
                    jnp.concatenate([vals[h * 8 + q][:, :128], vals[h * 8 + q][:, 128:]], axis=0).astype(jnp.bfloat16)
                    for q in range(8)
                ]
                for q, tile in enumerate(swap_blocks(packed)):
                    lhs[pl.ds((ti * 8 + q) * 16, 16), pl.ds(k * 256 + h * 128, 128)] = tile


def send_kernel(
    tab_in, lhs_in, lab, from_c, from_x, from_a, from_b, diff, bank, out,
    tab, lhs, prod, owns, pairs, sides, corners, sems,
):
    copies = [pltpu.make_async_copy(src, dst, sems.at[n]) for n, (src, dst) in enumerate(((tab_in, tab), (lhs_in, lhs)))]
    for copy in copies:
        copy.start()
    lane = lanes((8, 128))
    sub = lax.broadcasted_iota(jnp.int32, (8, 128), 0)
    a_of, b_of = lane // 16, lane % 16
    is_label = (a_of == 2) & (b_of >= 4) & (b_of < 12) | (a_of == 3) & (b_of >= 4) & (b_of < 6)
    absent = jnp.where(is_label, ABSENT, 0.0)
    offset = (sub - 1).astype(jnp.float32)

    zero = jnp.zeros((8, 128), jnp.float32)

    def clear(o, carry):
        at = pl.multiple_of(o * 16, 16)
        half = pl.multiple_of(o * 8, 8)
        owns[pl.ds(at, 8), :] = zero
        owns[pl.ds(at + 8, 8), :] = zero
        pairs[pl.ds(half, 8), :] = zero
        sides[pl.ds(half, 8), :] = zero
        corners[pl.ds(at, 8), :] = zero
        corners[pl.ds(at + 8, 8), :] = zero
        return carry

    lax.fori_loop(0, OWNERS, clear, 0, unroll=16)
    for copy in copies:
        copy.wait()

    above, below, before, after = sides_of(from_c, from_x, from_a, from_b)
    lane16 = lanes((16, 128))

    def add(ti, q, k, h, lo, hi, what):
        rows_at, cols_at = pl.ds((ti * 8 + q) * 16, 16), pl.ds(k * 256 + h * 128, 128)
        if hi - lo == 8:
            none = jnp.zeros((8, 128), jnp.float32)
            what = jnp.concatenate([what, none] if lo == 0 else [none, what], axis=0)
        lhs[rows_at, cols_at] = (lhs[rows_at, cols_at].astype(jnp.float32) + what).astype(jnp.bfloat16)

    top, bottom = above(0, 16) * -0.5, below(0, 16) * 0.5
    for q in range(8):
        add(0, q, 1, 0, 0, 16, jnp.where(lane16 < 16, pltpu.roll(top, (128 - 16 * q) % 128, 1), 0.0))
        add(3, q, 1, 1, 0, 16, jnp.where(lane16 >= 112, pltpu.roll(bottom, 112 - 16 * q, 1), 0.0))
    left, right = before(0, 8) * -0.5, after(0, 8) * 0.5
    for ti in range(4):
        for h in range(2):
            low = jnp.zeros((8, 128), jnp.float32)
            high = jnp.zeros((8, 128), jnp.float32)
            for q in range(8):
                i = ti * 16 + h * 8 + q
                low = jnp.where(lane == q * 16, left[:, i : i + 1], low)
                high = jnp.where(lane == q * 16 + 15, right[:, i : i + 1], high)
            add(ti, 0, 2, h, 0, 8, low)
            add(ti, 7, 2, h, 8, 16, high)

    def product(n, carry):
        rhs = jnp.concatenate([bank[2 * n], bank[2 * n + 1]], axis=1)
        res = jnp.dot(lhs[...], rhs, preferred_element_type=jnp.float32)
        at = pl.multiple_of(n * 1024, 1024)
        prod[pl.ds(at, 512), :] = res[:, :128]
        prod[pl.ds(at + 512, 512), :] = res[:, 128:]
        return carry

    lax.fori_loop(0, NWB // 2, product, 0, unroll=8)

    half_of, quarter_of = lane // 64, b_of // 4
    code = half_of * 4 + quarter_of

    def rows(ref, at):
        return ref.at[pl.ds(pl.multiple_of(at, 8), 8), :]

    for r in range(RECS):
        value = rows(prod, tab[PROD, r])[...]
        rows(owns, tab[OWN, r])[...] = value
        pltpu.store(rows(pairs, tab[XROW, r]), pltpu.roll(value, tab[XTURN, r], 1), mask=half_of == tab[KX, r])
        pltpu.store(rows(sides, tab[YROW, r]), pltpu.roll(value, tab[SHIFT, r], 1), mask=quarter_of == tab[YQ, r])
        pltpu.store(rows(corners, tab[CROW, r]), value, mask=code == tab[CC, r])

    for du, dv in CORNERS:
        first = 0 if du < 0 else 24
        cells = diff[first : first + 8, :]
        high = cells.astype(jnp.bfloat16).astype(jnp.float32)
        low = cells - high
        to = rows(corners, neighbour(du, dv) * 16)
        if dv < 0:
            pltpu.store(to, pltpu.roll(high, 4, 1), mask=(lane >= 4) & (lane < 8))
            pltpu.store(to, pltpu.roll(low, 8, 1), mask=(lane >= 8) & (lane < 12))
        else:
            pltpu.store(to, pltpu.roll(high, 124, 1), mask=(lane >= 120) & (lane < 124))
            pltpu.store(to, pltpu.roll(low, 120, 1), mask=(lane >= 116) & (lane < 120))

    def convert(o, carry):
        at = pl.multiple_of(o * 16, 16)
        half = pl.ds(pl.multiple_of(o * 8, 8), 8)
        found = jnp.broadcast_to(lab[pl.ds(o, 1), :], (8, 128))
        tags = jnp.where(found > 0, found + offset, absent)
        last = tags + (corners[pl.ds(at, 8), :] + corners[pl.ds(at + 8, 8), :])
        out[o, 0:16, :] = owns[pl.ds(at, 16), :].astype(jnp.bfloat16)
        out[o, 16:32, :] = jnp.concatenate([pairs[half, :], sides[half, :]], axis=0).astype(jnp.bfloat16)
        out[o, 32:40, :] = last.astype(jnp.bfloat16)
        return carry

    lax.fori_loop(0, OWNERS, convert, 0, unroll=16)


def gather_kernel(recv, diff, from_c, from_x, from_a, from_b, centre, cross, swap, dext, onehot):
    lane = lanes((8, 128))
    b_of = lane % 16
    K = OWNERS * 16
    even_x = even("gx")
    own_in = recv[:, 0:16, :].reshape(K, 128)
    pair_in = recv[:, 16:32, :].reshape(K, 128)
    last = recv[:, 32:40, :].astype(jnp.float32)
    side_in = jnp.concatenate([jnp.zeros_like(last), last], axis=1).reshape(K, 128).astype(jnp.bfloat16)

    pick_row = lax.broadcasted_iota(jnp.int32, (16, 128), 0)
    pick_lane = lanes((16, 128))
    label_lane = jnp.where(pick_row < 8, 36 + pick_row, 44 + pick_row)
    pick = ((label_lane == pick_lane) & (pick_row < 10)).astype(jnp.float32).astype(jnp.bfloat16)
    keys = lax.dot_general(pick, side_in, (((1,), (1,)), ((), ())), preferred_element_type=jnp.float32)
    early = pltpu.roll(keys, K - 8, 1)
    klane = lanes((8, K))
    sub = lax.broadcasted_iota(jnp.int32, (8, K), 0).astype(jnp.float32)
    late = (klane & 8) != 0

    def spread(rows, at):
        return jnp.broadcast_to(rows[at : at + 1, :], (8, K))

    def both(at):
        return jnp.where(late, spread(keys, at + 1), spread(early, at)) - sub

    def first(row):
        return jnp.where(late, -1000.0, jnp.broadcast_to(row, (8, K))) - sub

    def second(at):
        return jnp.where(late, spread(keys, at), -1000.0) - sub

    def hot(base, key, count):
        for t in range(0, count, 2):
            pair = [jnp.where(key == 8.0 * (t + q), 1.0, 0.0) for q in range(2)]
            onehot[pl.ds(base + t * 8, 16), :] = jnp.concatenate(pair, axis=0).astype(jnp.bfloat16)

    hot(0, both(0), 32)
    for c in range(2):
        hot(256 + 64 * c, first(jnp.where(even_x, early[4 + c : 5 + c, :], early[2 + c : 3 + c, :])), 8)
    for c in range(4):
        hot(384 + 32 * c, second(6 + c), 4)
    hot(512, jnp.where(late, (klane & 7).astype(jnp.float32), -1000.0) - sub, 2)

    def dot(lo, hi, rhs):
        return jnp.dot(onehot[lo:hi, :], rhs, preferred_element_type=jnp.float32)

    own = dot(0, 256, own_in)
    beside = dot(256, 512, pair_in)
    pairs, sides = beside[0:128, :], beside[128:256, :]
    corners = dot(512, 528, side_in)

    def tile(x, at):
        return x[at * 8 : at * 8 + 8, :]

    def side_rows(cells):
        turned = [pltpu.roll(cells, (128 - 16 * a) % 128, 1) if a % 8 else cells for a in range(8)]
        return [jnp.where(lane < 4, turned[a], jnp.where(lane >= 124, turned[(a + 1) % 8], 0.0)) for a in range(8)]

    for tx in range(4):
        rows = swap_blocks([tile(own, tx * 8 + ty) for ty in range(8)])
        r = tile(sides, tx) + pltpu.roll(tile(sides, 4 + tx), 124, 1)
        l = tile(sides, 8 + tx) + pltpu.roll(tile(sides, 12 + tx), 4, 1)
        ends_of = side_rows(jnp.where(b_of < 4, r, l))
        for a in range(8):
            centre[tx * 8 + a] = jnp.concatenate([rows[a], ends_of[a]], axis=1)
    rows = swap_blocks([tile(pairs, ty) + pltpu.roll(tile(pairs, 8 + ty), 64, 1) for ty in range(8)])
    ends_of = side_rows(tile(corners, 0))
    for a in range(4):
        cross[a] = jnp.concatenate(
            [jnp.where(even_x, rows[4 + a], rows[a]), jnp.where(even_x, ends_of[4 + a], ends_of[a])], axis=1
        )
        swap[a] = jnp.where(even_x, centre[28 + a], centre[a])

    above, below, before, after = sides_of(from_c, from_x, from_a, from_b)

    def flag(du, dv):
        return jnp.where(neighbour(du, dv) < OWNERS, 1.0, 0.0)

    def corner(du, dv):
        s = neighbour(du, dv)
        z = recv[jnp.minimum(s, OWNERS - 1), 32:40, :].astype(jnp.float32)
        z = jnp.where(s < OWNERS, z, 0.0)
        left = pltpu.roll(z, 4, 1) + pltpu.roll(z, 8, 1)
        right = pltpu.roll(z, 124, 1) + pltpu.roll(z, 120, 1)
        return left if dv < 0 else right

    def ends(left, right):
        return jnp.where(lane < 4, right, jnp.where(lane >= 124, left, 0.0))

    dext[0:8, 0:128] = above(40, 48) * flag(-1, 0)
    dext[40:48, 0:128] = below(16, 24) * flag(1, 0)
    dext[8:40, 0:128] = diff[...]
    dext[0:8, 128:256] = ends(corner(-1, -1), corner(-1, 1))
    dext[40:48, 128:256] = ends(corner(1, -1), corner(1, 1))
    for q in range(4):
        dext[8 + q * 8 : 16 + q * 8, 128:256] = ends(
            before(8 + q * 8, 16 + q * 8) * flag(0, -1), after(8 + q * 8, 16 + q * 8) * flag(0, 1)
        )


def sweep_kernel(centre, cross, swapped, dext, out, u0, u1):
    even_x = even("gx")
    for a in range(4):
        u0[a] = jnp.where(even_x, cross[a], swapped[a])
        u0[36 + a] = jnp.where(even_x, swapped[a], cross[a])

    def start(e):
        return u0[e] if e < 4 or e >= 36 else centre[e - 4]

    ping, pong = u1.at[0], u1.at[1]
    for sweep in range(SWEEPS):
        dst = pong if sweep % 2 else ping
        src = ping if sweep % 2 else pong
        for e in range(sweep + 1, 39 - sweep):
            at = start if sweep == 0 else lambda n, src=src: src[n]
            u = at(e)
            beside = at(e + 1) + at(e - 1) + pltpu.roll(u, 255, 1) + pltpu.roll(u, 1, 1)
            d = jnp.broadcast_to(dext[e + 4 : e + 5, :], (8, 256))
            new = u + d * (beside - 4.0 * u)
            if sweep < SWEEPS - 1:
                dst[e] = new
            else:
                out[pl.ds(e - 4, 8, stride=OXD), :] = new[:, :128]


def local(flux, diffusivity, remap_bank, rec_owner, rec_source, rec_target, rec_weight):
    vmem = pl.BlockSpec(memory_space=pltpu.VMEM)
    smem = pl.BlockSpec(memory_space=pltpu.SMEM)
    anywhere = pl.BlockSpec(memory_space=pl.ANY)
    flux_rows = flux.reshape(F * AXD, AYD)
    hbm = pl.BlockSpec(memory_space=pltpu.HBM)
    records = [x.reshape(1, RECS) for x in (rec_owner, rec_source, rec_target, rec_weight)]
    loads = [pltpu.with_memory_space_constraint(x, pltpu.HBM) for x in (flux_rows, diffusivity, *records)]
    f32, i32 = jnp.float32, jnp.int32
    to_c, to_x, to_a, to_b, tab, flux_halves, diff = pl.pallas_call(
        prepare_kernel,
        out_shape=[jax.ShapeDtypeStruct((48, 128), f32)] * 2
        + [jax.ShapeDtypeStruct((40, 128), f32)] * 2
        + [jax.ShapeDtypeStruct((TAB_ROWS, RECS), i32), jax.ShapeDtypeStruct((2, F * AXD, 128), f32)]
        + [jax.ShapeDtypeStruct((OXD, OYD), f32)],
        in_specs=[hbm] * 6,
        out_specs=[vmem] * 7,
        scratch_shapes=[pltpu.VMEM((4, 1, RECS), i32), pltpu.SemaphoreType.DMA((7,))],
        name="prepare",
        cost_estimate=pl.CostEstimate(flops=3000000000, bytes_accessed=8000000, transcendentals=0),
        compiler_params=pltpu.CompilerParams(vmem_limit_bytes=6 << 20),
    )(*loads)

    def swap(x, axis, count, odd):
        return lax.ppermute(x, axis, [(i, (((i + odd) ^ 1) - odd) % count) for i in range(count)])

    came = []
    for x, axis, count, odd in ((to_c, "gx", NGX, 0), (to_x, "gx", NGX, 1), (to_a, "gy", NGY, 0), (to_b, "gy", NGY, 1)):
        came.append(swap(x, axis, count, odd))

    bf16 = jnp.bfloat16
    lhs, lab = pl.pallas_call(
        tiles_kernel,
        out_shape=[jax.ShapeDtypeStruct((512, 768), bf16), jax.ShapeDtypeStruct((OWNERS, 128), f32)],
        in_specs=[vmem] * 2,
        out_specs=[vmem] * 2,
        name="tiles",
    cost_estimate=pl.CostEstimate(flops=3000000000, bytes_accessed=8000000, transcendentals=0),
    compiler_params=pltpu.CompilerParams(vmem_limit_bytes=8 << 20),
    )(flux_halves, tab)

    outgoing = pl.pallas_call(
        send_kernel,
        out_shape=jax.ShapeDtypeStruct((OWNERS, 40, 128), bf16),
        in_specs=[anywhere] * 2 + [vmem] * 7,
        out_specs=vmem,
        scratch_shapes=[
            pltpu.SMEM((TAB_ROWS, RECS), i32),
            pltpu.VMEM((512, 768), bf16),
            pltpu.VMEM((NWB * 512, 128), f32),
            pltpu.VMEM((OWNERS * 16, 128), f32),
            pltpu.VMEM((OWNERS * 8 + 8, 128), f32),
            pltpu.VMEM((OWNERS * 8 + 8, 128), f32),
            pltpu.VMEM((OWNERS * 16 + 16, 128), f32),
            pltpu.SemaphoreType.DMA((2,)),
        ],
        name="remap_send",
        cost_estimate=pl.CostEstimate(flops=5000000000, bytes_accessed=8000000, transcendentals=0),
        compiler_params=pltpu.CompilerParams(vmem_limit_bytes=24 << 20),
    )(tab, lhs, lab, *came, diff, remap_bank.reshape(NWB, 768, 128))
    arrived = lax.all_to_all(outgoing, ("gx", "gy"), split_axis=0, concat_axis=0, tiled=True)
    shapes = [(OXD, 8, 256), (4, 8, 256), (4, 8, 256), (48, 256)]
    centre, cross, edge, dext = pl.pallas_call(
        gather_kernel,
        out_shape=[jax.ShapeDtypeStruct(shape, f32) for shape in shapes],
        in_specs=[vmem] * 6,
        out_specs=[vmem] * 4,
        scratch_shapes=[pltpu.VMEM((528, OWNERS * 16), bf16)],
        name="gather",
        cost_estimate=pl.CostEstimate(flops=3000000000, bytes_accessed=4000000, transcendentals=0),
        compiler_params=pltpu.CompilerParams(vmem_limit_bytes=16 << 20),
    )(arrived, diff, *came)
    edge = swap(edge, "gx", NGX, 0)
    ocean = pl.pallas_call(
        sweep_kernel,
        out_shape=jax.ShapeDtypeStruct((F * OXD, OYD), f32),
        in_specs=[vmem] * 4,
        out_specs=vmem,
        scratch_shapes=[pltpu.VMEM((40, 8, 256), f32), pltpu.VMEM((2, 40, 8, 256), f32)],
        name="sweeps",
        cost_estimate=pl.CostEstimate(flops=3000000000, bytes_accessed=4000000, transcendentals=0),
        compiler_params=pltpu.CompilerParams(vmem_limit_bytes=16 << 20),
    )(centre, cross, edge, dext)
    return ocean.reshape(F, OXD, OYD)


def solution(mesh):
    in_specs = (
        P(None, "gx", "gy"),
        P("gx", "gy"),
        P(),
        P(("gx", "gy")),
        P(("gx", "gy")),
        P(("gx", "gy")),
        P(("gx", "gy")),
    )
    return jax.shard_map(local, mesh=mesh, in_specs=in_specs, out_specs=P(None, "gx", "gy"), check_vma=False)
```
